128 devices in a mesh: pts: 32 (over x, y, core), grp: 4 (over z).
Axes of the slice: x: 4, y: 4, z: 4, core: 2. Of those that a mesh axis runs over, the one named last changes fastest.
Arguments:
- points: bfloat16 [262144, 256], P(('pts', 'grp')), may hold values from -6 to 6
- cotangent: bfloat16 [262144, 256], P(('pts', 'grp')), may hold values from -24 to 24
- gain_one: float32 [256], replicated, may hold values from 0.25 to 1.75
- gain_two: float32 [256], replicated, may hold values from 0.25 to 1.75
- w_mid: bfloat16 [256, 256], replicated, may hold values from -0.375 to 0.375
- w_feat: bfloat16 [256, 256], replicated, may hold values from -0.375 to 0.375
- w_out: bfloat16 [256, 256], replicated, may hold values from -0.375 to 0.375
- w_up: bfloat16 [256, 1024], replicated, may hold values from -0.375 to 0.375
- w_down: bfloat16 [256, 1024], replicated, may hold values from -0.1875 to 0.1875
- w_slice: float32 [32, 32], replicated, as said below
- w_temp: float32 [32], replicated, may hold values from -2 to 2
- query_matrix: float32 [32, 32], replicated
- key_matrix: float32 [32, 32], replicated
- value_matrix: float32 [32, 32], replicated, may hold values from -1 to 1
Outputs:
- grad_points: bfloat16 [262144, 256], P(('pts', 'grp'))
- grad_mid: float32 [256, 256], replicated
- grad_feat: float32 [256, 256], replicated
- grad_out: float32 [256, 256], replicated
- grad_up: float32 [256, 1024], replicated
- grad_down: float32 [256, 1024], replicated
- grad_gain_one: float32 [256], replicated
- grad_gain_two: float32 [256], replicated
- grad_slice: float32 [32, 32], replicated
- grad_temp: float32 [32], replicated
- grad_query: float32 [32, 32], replicated
- grad_key: float32 [32, 32], replicated
- grad_value: float32 [32, 32], replicated
The draws below stay inside these ranges and needn't reach their ends.
Inputs may be any that keep to these rules, and one draw needn't show every extreme that they name: w_slice is a real matrix.
All inputs are finite; a program needn't handle non-finite values.
Results may differ from the reference program's by a relative error of at most 0.023.
The reference program's roundings to bfloat16 on the way count: a program that leaves them out, or rounds other values in their place, can miss the bound.
Values sent between devices are 32-bit elements; how exact they have to be, the bound alone decides.
A program may use at most 128 MiB of HBM per device.

```python
import jax
import jax.numpy as jnp
from jax import lax

C = 256
HEADS = 8
HEAD_DIM = 32
SLICES = 32
FF = 1024
PTS_DEV = 2048
POINTS = 262144


def key_base(key):
    return jax.random.normal(jax.random.fold_in(key, 11), (HEAD_DIM, HEAD_DIM), jnp.float32)


def draw_key_matrix(key, part):
    return key_base(key) * HEAD_DIM ** (-0.5)


def draw_query_matrix(key, part):
    fresh = jax.random.normal(jax.random.fold_in(key, 12), (HEAD_DIM, HEAD_DIM), jnp.float32) * HEAD_DIM ** (-0.5)
    return 2.0 * fresh


def draw_w_slice(key, part):
    scale = 3.0 * HEAD_DIM ** (-0.5)
    return jax.random.normal(jax.random.fold_in(key, 25), (HEAD_DIM, SLICES), jnp.float32) * scale


def with_spikes(drawn, own_key, source, target, blocks, factor):
    def block_of(position):
        return (jnp.arange(drawn.shape[position]) // (drawn.shape[position] // blocks)).reshape((-1,) + (1,) * (drawn.ndim - 1 - position))

    first = jax.random.permutation(own_key, blocks)[block_of(target)]
    other_side = (block_of(target) + blocks // 2) % blocks
    return jnp.where((block_of(source) == first) | (block_of(source) == other_side), factor * drawn, drawn)


def block_scale(stream_key, dims, cuts, least, high):
    level, own = 1.0, jax.random.fold_in(stream_key, 6)
    for axis_at, shards_of in cuts:
        draws = jnp.exp(jax.random.uniform(jax.random.fold_in(own, axis_at), (shards_of,), jnp.float32, least / len(cuts), high / len(cuts)))
        level = level * jnp.repeat(draws, dims[axis_at] // shards_of).reshape([-1 if axis == axis_at else 1 for axis in range(len(dims))])
    return level


def noise(key, dims, width, limit, shards=(), kind=jnp.bfloat16):
    level = block_scale(key, dims, shards, -0.22, 0.18) if shards else 1.0
    values = jax.random.normal(key, dims, jnp.float32) * width * level
    return jnp.minimum(jnp.maximum(values, -limit), limit).astype(kind)


def gaussian_with(rng, shape, spread, limit, shards, heavy, held_as=jnp.bfloat16):
    values = spread * jax.random.normal(rng, shape, jnp.float32)
    if shards:
        values = values * block_scale(rng, shape, shards, -0.22, 0.18)
    return jnp.clip(with_spikes(values, jax.random.fold_in(rng, 3), *heavy), -limit, limit).astype(held_as)


def setup_inputs(seed: int = 0) -> dict:
    keys = jax.random.split(jax.random.key(seed), 15)
    points = noise(keys[0], (POINTS, C), 1.0, 6.0, ((0, 128),))
    cotangent = gaussian_with(keys[1], (POINTS, C), 1.0, 24.0, ((0, 128),), (0, 1, 128, 5.5))
    gain_one = jnp.clip(1.0 + 0.15 * jax.random.normal(keys[2], (C,), jnp.float32), 0.25, 1.75)
    gain_two = jnp.clip(1.0 + 0.15 * jax.random.normal(keys[3], (C,), jnp.float32), 0.25, 1.75)
    w_mid = noise(keys[4], (C, C), C ** -0.5, 0.375)
    w_feat = noise(keys[5], (C, C), C ** -0.5, 0.375)
    w_out = noise(keys[6], (C, C), C ** -0.5, 0.375)
    w_up = noise(keys[7], (C, FF), C ** -0.5, 0.375)
    w_down = noise(keys[8], (C, FF), FF ** -0.5, 0.1875)
    w_slice = draw_w_slice(jax.random.fold_in(keys[14], 71), 0)
    w_temp = noise(keys[10], (HEAD_DIM,), 0.3, 2.0, (), jnp.float32)
    query_matrix = draw_query_matrix(jax.random.fold_in(keys[14], 71), 0)
    key_matrix = draw_key_matrix(jax.random.fold_in(keys[14], 71), 0)
    value_matrix = noise(keys[13], (HEAD_DIM, HEAD_DIM), HEAD_DIM ** -0.5, 1.0, (), jnp.float32)
    return {"points": points, "cotangent": cotangent, "gain_one": gain_one, "gain_two": gain_two, "w_mid": w_mid, "w_feat": w_feat, "w_out": w_out, "w_up": w_up, "w_down": w_down, "w_slice": w_slice, "w_temp": w_temp, "query_matrix": query_matrix, "key_matrix": key_matrix, "value_matrix": value_matrix}


EPS_NORM = 1e-05
EPS_SLICE = 1e-05
PRECISION_LEVEL = lax.Precision.HIGHEST

def layer_norm(value_rows, gain):
    centred = value_rows - lax.optimization_barrier(jnp.mean(value_rows, axis=-1, keepdims=True))
    spread_tokens = lax.optimization_barrier(jnp.mean(centred * centred, axis=-1, keepdims=True))
    return centred * lax.rsqrt(spread_tokens + EPS_NORM) * gain

def assign(middle, w_slice, w_temp):
    temper = 0.5 + jax.nn.softplus(jnp.einsum('nhd,d->nh', middle, w_temp, precision=PRECISION_LEVEL))
    logits = jnp.einsum('nhd,dm->nhm', middle, w_slice, precision=PRECISION_LEVEL) / temper[:, :, None]
    return jax.nn.softmax(logits, axis=-1)

def mix_tokens(numerator_sums, denom, query_matrix, key_matrix, value_matrix):
    slice_token_rows = numerator_sums / (denom[:, :, None] + EPS_SLICE)
    query_rows = jnp.einsum('xsf,fz->xsz', slice_token_rows, query_matrix, precision=PRECISION_LEVEL)
    key_rows = jnp.einsum('xsf,fz->xsz', slice_token_rows, key_matrix, precision=PRECISION_LEVEL)
    value_rows = jnp.einsum('xsf,fz->xsz', slice_token_rows, value_matrix, precision=PRECISION_LEVEL)
    scores = jnp.einsum('hme,hne->hmn', query_rows, key_rows, precision=PRECISION_LEVEL) * slice_token_rows.shape[-1] ** (-0.5)
    probs = jax.nn.softmax(scores, axis=-1)
    return jnp.einsum('hmn,hne->hme', probs, value_rows, precision=PRECISION_LEVEL)

def front(block, gain_one, w_mid, w_feat, w_slice, w_temp):
    rows = block.shape[0]
    normed = layer_norm(block.astype(jnp.float32), gain_one).astype(jnp.bfloat16)
    middle = jnp.dot(normed, w_mid, preferred_element_type=jnp.float32).astype(jnp.bfloat16)
    feats = jnp.dot(normed, w_feat, preferred_element_type=jnp.float32).astype(jnp.bfloat16)
    weights = assign(middle.astype(jnp.float32).reshape(rows, HEADS, HEAD_DIM), w_slice, w_temp)
    return (normed, middle, feats, weights, weights.astype(jnp.bfloat16))

def rear(block, cot, weight_rows_low, mixed_token_low, w_out, gain_two, w_up, w_down):
    rows = block.shape[0]
    spread_tokens = jnp.einsum('lge,gex->lgx', weight_rows_low.astype(jnp.float32), mixed_token_low.astype(jnp.float32))
    spread_tokens = spread_tokens.astype(jnp.bfloat16).reshape(rows, C)
    resid = (block.astype(jnp.float32) + jnp.dot(spread_tokens, w_out, preferred_element_type=jnp.float32)).astype(jnp.bfloat16)
    resid_f = resid.astype(jnp.float32)
    normed_two = layer_norm(resid_f, gain_two).astype(jnp.bfloat16)
    pre = jnp.dot(normed_two, w_up, preferred_element_type=jnp.float32)
    hidden = jax.nn.gelu(pre).astype(jnp.bfloat16)
    d_hid = jnp.dot(cot, w_down, preferred_element_type=jnp.float32)
    gelu_back = jax.vjp(jax.nn.gelu, pre)[1]
    d_pre = gelu_back(d_hid)[0].astype(jnp.bfloat16)
    d_norm_two = lax.dot_general(d_pre, w_up, (((1,), (1,)), ((), ())), preferred_element_type=jnp.float32)
    norm_back = jax.vjp(layer_norm, resid_f, gain_two)[1]
    d_res_ln, d_gain_two = norm_back(d_norm_two)
    d_resid = cot.astype(jnp.float32) + d_res_ln
    d_resid_b = d_resid.astype(jnp.bfloat16)
    spread_gradient = lax.dot_general(d_resid_b, w_out, (((1,), (1,)), ((), ())), preferred_element_type=jnp.float32)
    spread_gradient = spread_gradient.astype(jnp.bfloat16).reshape(rows, HEADS, HEAD_DIM)
    return (spread_tokens, normed_two, hidden, d_pre, d_resid, d_resid_b, spread_gradient, d_gain_two)

def finish(block, middle, feats, weight_rows_low, mixed_token_low, d_resid, spread_gradient, numerator_gradient, denominator_gradient, w_mid, w_feat, gain_one, w_slice, w_temp):
    rows = block.shape[0]
    feature_rows_float = feats.astype(jnp.float32).reshape(rows, HEADS, HEAD_DIM)
    weight_gradient = jnp.einsum('wkt,klt->wkl', spread_gradient.astype(jnp.float32), mixed_token_low.astype(jnp.float32))
    weight_gradient = weight_gradient + jnp.einsum('wkt,klt->wkl', feature_rows_float, numerator_gradient) + denominator_gradient[None, :, :]
    feature_gradient = jnp.einsum('lge,gex->lgx', weight_rows_low.astype(jnp.float32), numerator_gradient)
    feature_gradient = feature_gradient.astype(jnp.bfloat16).reshape(rows, C)
    assign_back = jax.vjp(assign, middle.astype(jnp.float32).reshape(rows, HEADS, HEAD_DIM), w_slice, w_temp)[1]
    d_mid, d_slice, d_temp = assign_back(weight_gradient)
    d_mid = d_mid.reshape(rows, C).astype(jnp.bfloat16)
    d_normed = lax.dot_general(d_mid, w_mid, (((1,), (1,)), ((), ())), preferred_element_type=jnp.float32)
    d_normed = d_normed + lax.dot_general(feature_gradient, w_feat, (((1,), (1,)), ((), ())), preferred_element_type=jnp.float32)
    norm_back = jax.vjp(layer_norm, block.astype(jnp.float32), gain_one)[1]
    d_ln, d_gain_one = norm_back(d_normed)
    grad_block = (d_resid + d_ln).astype(jnp.bfloat16)
    return (grad_block, d_mid, feature_gradient, d_slice, d_temp, d_gain_one)

def transposed(left, right):
    return lax.dot_general(left, right, (((0,), (0,)), ((), ())), preferred_element_type=jnp.float32)

def reference(points, cotangent, gain_one, gain_two, w_mid, w_feat, w_out, w_up, w_down, w_slice, w_temp, query_matrix, key_matrix, value_matrix):
    blocks = points.shape[0] // PTS_DEV
    point_blocks = points.reshape(blocks, PTS_DEV, C)
    cot_blocks = cotangent.reshape(blocks, PTS_DEV, C)

    def first_pass(loop_carried, block):
        normed, middle, feats, weights, weight_rows_low = front(block, gain_one, w_mid, w_feat, w_slice, w_temp)
        feature_rows_float = feats.astype(jnp.float32).reshape(PTS_DEV, HEADS, HEAD_DIM)
        numerator_sums = loop_carried[0] + jnp.einsum('gux,guj->uxj', weight_rows_low.astype(jnp.float32), feature_rows_float)
        denom = loop_carried[1] + lax.optimization_barrier(jnp.sum(weights, axis=0))
        return ((numerator_sums, denom), None)
    start = (jnp.zeros((HEADS, SLICES, HEAD_DIM), jnp.float32), jnp.zeros((HEADS, SLICES), jnp.float32))
    (numerator_sums, denom), _ = lax.scan(first_pass, start, point_blocks)
    mixed_token_low = mix_tokens(numerator_sums, denom, query_matrix, key_matrix, value_matrix).astype(jnp.bfloat16)

    def second_pass(loop_carried, pair):
        block, cot = pair
        normed, middle, feats, weights, weight_rows_low = front(block, gain_one, w_mid, w_feat, w_slice, w_temp)
        outs = rear(block, cot, weight_rows_low, mixed_token_low, w_out, gain_two, w_up, w_down)
        spread_gradient = outs[6]
        return (loop_carried + jnp.einsum('gux,guj->uxj', weight_rows_low.astype(jnp.float32), spread_gradient.astype(jnp.float32)), None)
    mixed_gradient, _ = lax.scan(second_pass, jnp.zeros((HEADS, SLICES, HEAD_DIM), jnp.float32), (point_blocks, cot_blocks))
    token_back = jax.vjp(mix_tokens, numerator_sums, denom, query_matrix, key_matrix, value_matrix)[1]
    numerator_gradient, denominator_gradient, grad_query, grad_key, grad_value = token_back(mixed_gradient)

    def third_pass(loop_carried, pair):
        block, cot = pair
        normed, middle, feats, weights, weight_rows_low = front(block, gain_one, w_mid, w_feat, w_slice, w_temp)
        spread_tokens, normed_two, hidden, d_pre, d_resid, d_resid_b, spread_gradient, d_gain_two = rear(block, cot, weight_rows_low, mixed_token_low, w_out, gain_two, w_up, w_down)
        grad_block, d_mid, feature_gradient, d_slice, d_temp, d_gain_one = finish(block, middle, feats, weight_rows_low, mixed_token_low, d_resid, spread_gradient, numerator_gradient, denominator_gradient, w_mid, w_feat, gain_one, w_slice, w_temp)
        terms = jnp.concatenate([transposed(normed, d_mid), transposed(normed, feature_gradient), transposed(spread_tokens, d_resid_b), transposed(normed_two, d_pre), transposed(cot, hidden)], axis=1)
        big, g_slice, g_temp, g_one, g_two = loop_carried
        return ((big + terms, g_slice + d_slice, g_temp + d_temp, g_one + d_gain_one, g_two + d_gain_two), grad_block)
    start = (jnp.zeros((C, 3 * C + 2 * FF), jnp.float32), jnp.zeros((HEAD_DIM, SLICES), jnp.float32), jnp.zeros((HEAD_DIM,), jnp.float32), jnp.zeros((C,), jnp.float32), jnp.zeros((C,), jnp.float32))
    (big, g_slice, g_temp, g_one, g_two), grad_blocks = lax.scan(third_pass, start, (point_blocks, cot_blocks))
    grad_points = grad_blocks.reshape(blocks * PTS_DEV, C)
    return (grad_points, big[:, :C], big[:, C:2 * C], big[:, 2 * C:3 * C], big[:, 3 * C:3 * C + FF], big[:, 3 * C + FF:], g_one, g_two, g_slice, g_temp, grad_query, grad_key, grad_value)
```

```python
import jax
import jax.numpy as jnp
from jax import lax
from jax.experimental import pallas as pl
from jax.experimental.pallas import tpu as pltpu
from jax.sharding import PartitionSpec as P

F32 = jnp.float32
BF = jnp.bfloat16
MESH = pl.DeviceIdType.MESH
EXACT = lax.Precision.HIGHEST
C = 256
HEADS = 8
FF = 1024
NB = 512
EPS = 1e-5
K0 = 0.7978845608028654
K1 = K0 * 0.044715
ROWS_S = 72
PART_S = 24
ROWS_G = 4608
ROWS_T = 1152


def dg(a, b, ca, cb, precision=None):
    return lax.dot_general(
        a, b, (((ca,), (cb,)), ((), ())), precision=precision, preferred_element_type=F32
    )


def split3(v):
    hi = v.astype(BF)
    rest = v - hi.astype(F32)
    mid = rest.astype(BF)
    low = (rest - mid.astype(F32)).astype(BF)
    return hi, mid, low


def split2(v):
    hi = v.astype(BF)
    return hi, (v - hi.astype(F32)).astype(BF)


def iota(shape, dim):
    return lax.broadcasted_iota(jnp.int32, shape, dim)


def same_block(rows, cols):
    return (iota((rows, cols), 0) // 32) == (iota((rows, cols), 1) // 32)


def one_hot_rows(rows):
    return ((iota((rows, 32), 0) % 32) == iota((rows, 32), 1)).astype(F32)


def lanes4(col):
    return jnp.concatenate([col] * (NB // 128), axis=1)


def fold_lanes(v):
    out = v[:, 0:128]
    for j in range(1, v.shape[1] // 128):
        out = out + v[:, 128 * j : 128 * (j + 1)]
    return out


def column_to_rows(col):
    eye = iota((128, 128), 0) == iota((128, 128), 1)
    rows = []
    for a in range(col.shape[0] // 128):
        spread = jnp.broadcast_to(col[128 * a : 128 * (a + 1)], (128, 128))
        rows.append(jnp.sum(jnp.where(eye, spread, 0.0), axis=0, keepdims=True))
    return rows


def fold_diagonal(full):
    parts = []
    mask = same_block(128, 128)
    for a in range(2):
        sub = jnp.where(mask, full[128 * a : 128 * (a + 1), 128 * a : 128 * (a + 1)], 0.0)
        parts.append(sub[0:32] + sub[32:64] + sub[64:96] + sub[96:128])
    return jnp.concatenate(parts, axis=0)


def tile_diagonal(compact):
    return jnp.where(same_block(128, 128), jnp.concatenate([compact] * 4, axis=0), 0.0)


class Net:
    def __init__(self, send_sems, recv_sems, active):
        self.send_sems, self.recv_sems, self.active = send_sems, recv_sems, active
        self.count, self.open = 0, []
        if active:
            pts, z = lax.axis_index("pts"), lax.axis_index("grp")
            core, y, x = pts % 2, (pts // 2) % 4, pts // 8
            self.core = core
            self.at = (x, y, z)
            self.partner = (pts + 1 - 2 * core, z)
            self.peer = (
                lambda j: (j * 8 + y * 2 + core, z),
                lambda j: (x * 8 + j * 2 + core, z),
                lambda j: (pts, j),
            )

    def hello(self):
        if not self.active:
            return
        barrier = pltpu.get_barrier_semaphore()
        pl.semaphore_signal(barrier, inc=1, device_id=self.partner, device_id_type=MESH)
        for ax in range(3):
            for d in range(1, 4):
                pl.semaphore_signal(
                    barrier,
                    inc=1,
                    device_id=self.peer[ax]((self.at[ax] + d) % 4),
                    device_id_type=MESH,
                )

    def ready(self):
        if self.active:
            pl.semaphore_wait(pltpu.get_barrier_semaphore(), 10)

    def send(self, src, dst, device):
        k = self.count
        self.count += 1
        copy = pltpu.make_async_remote_copy(
            src_ref=src,
            dst_ref=dst,
            send_sem=self.send_sems.at[k],
            recv_sem=self.recv_sems.at[k],
            device_id=device,
            device_id_type=MESH,
        )
        copy.start()
        self.open.append(copy)
        return copy

    def drain(self):
        for copy in self.open:
            copy.wait_send()
        self.open = []


def rows(start, size):
    return pl.ds(pl.multiple_of(start, 8), size)


def small_sum(net, src, from_core, slots, out):
    if not net.active:
        out[...] = src[...]
        return
    copy = net.send(src, from_core, net.partner)
    yield
    copy.wait_recv()
    parts = [
        src[PART_S * p : PART_S * (p + 1), :] + from_core[PART_S * p : PART_S * (p + 1), :]
        for p in range(3)
    ]
    for k in range(3):
        copies = []
        for p in range(3):
            ax = (p + k) % 3
            mine = rows(k * 12 * PART_S + (p * 4 + net.at[ax]) * PART_S, PART_S)
            slots[mine, :] = parts[p]
            for d in range(1, 4):
                copies.append(
                    net.send(slots.at[mine, :], slots.at[mine, :], net.peer[ax]((net.at[ax] + d) % 4))
                )
        yield
        for copy in copies:
            copy.wait_recv()
        for p in range(3):
            four = [
                slots[pl.ds(k * 12 * PART_S + (p * 4 + s) * PART_S, PART_S), :]
                for s in range(4)
            ]
            parts[p] = (four[0] + four[1]) + (four[2] + four[3])
    for p in range(3):
        out[PART_S * p : PART_S * (p + 1), :] = parts[p]


def core_scatter(net, src, got, summed, part, barrier_copies=None):
    half = part // 2
    copies = []
    for p in range(3):
        theirs = rows(p * part + (1 - net.core) * half, half)
        copies.append(net.send(src.at[theirs, :], got.at[pl.ds(p * half, half), :], net.partner))
    yield
    for p, copy in enumerate(copies):
        copy.wait_recv()
        here = pl.ds(p * half, half)
        summed[here, :] = src[rows(p * part + net.core * half, half), :] + got[here, :]


def axis_scatter(net, k, src, got, size, store):
    piece = size // 4
    copies = []
    for p in range(3):
        ax = (p + k) % 3
        for d in range(1, 4):
            j = (net.at[ax] + d) % 4
            copies.append(
                net.send(
                    src.at[rows(p * size + j * piece, piece), :],
                    got.at[pl.ds((p * 3 + d - 1) * piece, piece), :],
                    net.peer[ax](j),
                )
            )
    yield
    for copy in copies:
        copy.wait_recv()
    for p in range(3):
        ax = (p + k) % 3
        own = src[rows(p * size + net.at[ax] * piece, piece), :]
        three = [got[pl.ds((p * 3 + d) * piece, piece), :] for d in range(3)]
        store(p, (own + three[0]) + (three[1] + three[2]))


def axis_exchange(net, k, slots, size, store):
    copies = []
    for p in range(3):
        ax = (p + k) % 3
        mine = rows((p * 4 + net.at[ax]) * size, size)
        for d in range(1, 4):
            copies.append(
                net.send(slots.at[mine, :], slots.at[mine, :], net.peer[ax]((net.at[ax] + d) % 4))
            )
    yield
    for copy in copies:
        copy.wait_recv()
    for p in range(3):
        four = [slots[pl.ds((p * 4 + s) * size, size), :] for s in range(4)]
        store(p, (four[0] + four[1]) + (four[2] + four[3]))


def axis_gather(net, k, out, where):
    copies = []
    for p in range(3):
        ax = (p + k) % 3
        for d in range(1, 4):
            here = out.at[where(p), :]
            copies.append(net.send(here, here, net.peer[ax]((net.at[ax] + d) % 4)))
    yield
    for copy in copies:
        copy.wait_recv()


def core_gather(net, out, where):
    copies = [net.send(out.at[where(p), :], out.at[where(p), :], net.partner) for p in range(3)]
    yield
    for copy in copies:
        copy.wait_recv()


def bulk_sum(net, src, got0, sum0, got1, sum1, got2, slots, out):
    if not net.active:
        out[...] = src[...]
        return
    part, half, quarter, piece = 1536, 768, 192, 48
    yield from core_scatter(net, src, got0, sum0, part)

    def keep1(p, v):
        sum1[pl.ds(p * quarter, quarter), :] = v

    yield from axis_scatter(net, 0, sum0, got1, half, keep1)

    def keep2(p, v):
        slots[rows((p * 4 + net.at[(p + 2) % 3]) * piece, piece), :] = v

    yield from axis_scatter(net, 1, sum1, got2, quarter, keep2)

    def base(p, depth):
        at = p * part + net.core * half
        if depth > 0:
            at = at + net.at[p % 3] * quarter
        if depth > 1:
            at = at + net.at[(p + 1) % 3] * piece
        return at

    def keep3(p, v):
        out[rows(base(p, 2), piece), :] = v

    yield from axis_exchange(net, 2, slots, piece, keep3)
    yield from axis_gather(net, 1, out, lambda p: rows(base(p, 2), piece))
    yield from axis_gather(net, 0, out, lambda p: rows(base(p, 1), quarter))
    yield from core_gather(net, out, lambda p: rows(base(p, 0), half))


def tail_sum(net, src, got0, sum0, got1, slots1, slots2, out):
    if not net.active:
        out[...] = src[...]
        return
    part, half, piece = 384, 192, 48
    yield from core_scatter(net, src, got0, sum0, part)

    def keep(slots, k):
        def store(p, v):
            slots[rows((p * 4 + net.at[(p + k) % 3]) * piece, piece), :] = v

        return store

    yield from axis_scatter(net, 0, sum0, got1, half, keep(slots1, 1))
    yield from axis_exchange(net, 1, slots1, piece, keep(slots2, 2))

    def where(p, depth):
        at = p * part + net.core * half
        if depth > 0:
            at = at + net.at[p % 3] * piece
        return rows(at, piece if depth else half)

    def last(p, v):
        out[where(p, 1), :] = v

    yield from axis_exchange(net, 2, slots2, piece, last)
    yield from axis_gather(net, 0, out, lambda p: where(p, 1))
    yield from core_gather(net, out, lambda p: where(p, 0))


def step_of(gen):
    next(gen, None)


def finish_of(gen):
    for _ in gen:
        pass


def kernel(
    active,
    points_h, cot_h, w_mid_h, w_feat_h, w_out_h, w_up_h, w_down_h,
    gain_one, gain_two, w_slice, w_temp, w_q, w_k, w_v,
    o_points, o_mid, o_feat, o_out, o_up, o_down,
    o_one, o_two, o_slice, o_temp, o_q, o_k, o_v,
    pts_v, cot_v, wm_v, wf_v, wo_v, wu_v, wd_v,
    pT, cT, wmfT, wmf, woT, wuT, wdT,
    g1c, g2c, wtc, bds, bdd, bqkv,
    stat, nT, mfT, rts, sgs, ls, ws, wb, dacc,
    tok_s, qkv_s, prob_s, denb_s, mixT, lhs_c, dnT, ddc,
    dhT, sT, n2T, xh2, hT, dpT, drT, drb, dsT, ga1, ga2,
    dl_s, dt_s, dmf_s, gp_v,
    s1_src, s1_core, s1_slots, s1_out, s2_src, s2_core, s2_slots, s2_out,
    b_src, b_got0, b_sum0, b_got1, b_sum1, b_got2, b_slots, b_out,
    t_src, t_got0, t_sum0, t_got1, t_slots1, t_slots2, t_out,
    in_sems, out_sems, send_sems, recv_sems,
):
    n = pts_v.shape[0]
    chunks = n // NB
    net = Net(send_sems, recv_sems, active)
    net.hello()

    loads = [
        pltpu.make_async_copy(src, dst, in_sems.at[i])
        for i, (src, dst) in enumerate(
            [(w_mid_h, wm_v), (w_feat_h, wf_v), (points_h, pts_v), (cot_h, cot_v),
             (w_out_h, wo_v), (w_up_h, wu_v), (w_down_h, wd_v)]
        )
    ]
    for load in loads:
        load.start()

    hot = one_hot_rows(256)
    mask = same_block(256, 256)
    slice_t = jnp.where(mask, dg(dg(hot, w_slice[...], 1, 1, EXACT), hot, 1, 1, EXACT), 0.0)
    slice_n = jnp.where(mask, dg(dg(hot, w_slice[...], 1, 0, EXACT), hot, 1, 1, EXACT), 0.0)
    temp8 = jnp.where(
        iota((8, 256), 0) == iota((8, 256), 1) // 32,
        dg(jnp.broadcast_to(w_temp[...], (8, 32)), hot, 1, 1, EXACT),
        0.0,
    )
    wtc[...] = dg(hot, jnp.broadcast_to(w_temp[...], (128, 32)), 1, 1, EXACT)
    for i, v in enumerate(split3(slice_t)):
        bds[256 * i : 256 * (i + 1), :] = v
    t_hi = temp8.astype(BF).astype(F32)
    t_mid = (temp8 - t_hi).astype(BF).astype(F32)
    t_low = temp8 - t_hi - t_mid
    bds[768:800, :] = jnp.concatenate([t_hi, t_mid, t_low, jnp.zeros((8, 256), F32)], axis=0).astype(BF)
    n_hi, n_lo = split2(slice_n)
    bdd[:, 0:256] = n_hi
    bdd[:, 256:512] = n_hi
    bdd[:, 512:768] = n_lo
    g1c[...] = jnp.broadcast_to(gain_one[...], (128, 256)).T
    g2c[...] = jnp.broadcast_to(gain_two[...], (128, 256)).T
    hot4 = one_hot_rows(128)
    mask4 = same_block(128, 128)
    for i, w in enumerate((w_q, w_k, w_v)):
        bqkv[:, 128 * i : 128 * (i + 1)] = jnp.where(
            mask4, dg(dg(hot4, w[...], 1, 0, EXACT), hot4, 1, 1, EXACT), 0.0
        )
    dacc[...] = jnp.zeros_like(dacc)
    ga1[...] = jnp.zeros_like(ga1)
    ga2[...] = jnp.zeros_like(ga2)
    t_src[1024:ROWS_T, :] = jnp.zeros((ROWS_T - 1024, 128), F32)

    loads[0].wait()
    loads[1].wait()
    wmfT[0:256, :] = wm_v[...].T
    wmfT[256:512, :] = wf_v[...].T
    wmf[:, 0:256] = wm_v[...]
    wmf[:, 256:512] = wf_v[...]
    loads[2].wait()

    def front(i, _):
        s = pl.ds(pl.multiple_of(i * NB, NB), NB)
        xT = pts_v[s, :].T
        pT[:, s] = xT
        x = xT.astype(F32)
        mean = jnp.sum(x, axis=0, keepdims=True) * (1.0 / C)
        xc = x - mean
        var = jnp.sum(xc * xc, axis=0, keepdims=True) * (1.0 / C)
        rstd = lax.rsqrt(var + EPS)
        stat[0:1, s] = mean
        stat[1:2, s] = rstd
        normed = (xc * rstd * lanes4(g1c[...])).astype(BF)
        nT[:, s] = normed
        mf = dg(wmfT[...], normed, 1, 0).astype(BF)
        mfT[:, s] = mf
        lg = dg(bds[...], mf[0:256], 1, 0)
        t = lg[768:776] + lg[776:784] + lg[784:792]
        rt = 1.0 / (0.5 + (jnp.maximum(t, 0.0) + jnp.log(1.0 + jnp.exp(-jnp.abs(t)))))
        rts[:, s] = rt
        sgs[:, s] = 1.0 / (1.0 + jnp.exp(-t))
        for h in range(HEADS):
            r = slice(32 * h, 32 * h + 32)
            l = (lg[r] + lg[256 + 32 * h : 288 + 32 * h] + lg[512 + 32 * h : 544 + 32 * h]) * rt[h : h + 1]
            e = jnp.exp(l - jnp.max(l, axis=0, keepdims=True))
            w = e * (1.0 / jnp.sum(e, axis=0, keepdims=True))
            ls[r, s] = l
            ws[r, s] = w
            wb[r, s] = w.astype(BF)
            dacc[r, :] += fold_lanes(w)
        return 0

    lax.fori_loop(0, chunks, front, 0)
    s1_src[0:64, :] = fold_diagonal(dg(wb[...], mfT[256:512, :], 1, 1))
    den_rows = column_to_rows(jnp.sum(dacc[...], axis=1, keepdims=True))
    s1_src[64:72, :] = jnp.concatenate(den_rows + [jnp.zeros((6, 128), F32)], axis=0)

    net.ready()
    first = small_sum(net, s1_src, s1_core, s1_slots, s1_out)
    step_of(first)

    for i in range(3, 7):
        loads[i].wait()
    wdT[...] = wd_v[...].T

    def hidden_gradient(i):
        s = pl.ds(pl.multiple_of(i * NB, NB), NB)
        cT[:, s] = cot_v[s, :].T
        dhT[:, s] = dg(wdT[...], cT[:, s], 1, 0)

    for i in range(chunks):
        hidden_gradient(i)
        if i == 0:
            woT[...] = wo_v[...].T
            wuT[...] = wu_v[...].T
        step_of(first)
    finish_of(first)

    total = s1_out[0:64, :]
    picked = []
    pick = (iota((32, 128), 1) % 32) == iota((32, 128), 0)
    for a in range(2):
        picked.append(jnp.where(pick, jnp.broadcast_to(s1_out[64 + a : 65 + a, :], (32, 128)), 0.0))
    ones4 = mask4.astype(F32)
    denb = dg(jnp.concatenate(picked, axis=0), ones4, 1, 0, EXACT) + EPS
    denb_s[...] = denb
    tok = total / denb
    tok_s[...] = tok
    qkv = dg(tok, bqkv[...], 1, 0, EXACT)
    qkv_s[...] = qkv
    scale = 32.0 ** (-0.5)
    mixT[...] = jnp.zeros_like(mixT)
    lhs_c[...] = jnp.zeros_like(lhs_c)
    for a in range(2):
        r = slice(32 * a, 32 * a + 32)
        q_a, k_a, v_a = qkv[r, 0:128], qkv[r, 128:256], qkv[r, 256:384]
        sc = dg(k_a, tile_diagonal(q_a), 1, 1, EXACT) * scale
        e = jnp.exp(sc - jnp.max(sc, axis=0, keepdims=True))
        pr = e / jnp.sum(e, axis=0, keepdims=True)
        prob_s[r, :] = pr
        m_t = jnp.where(mask4, dg(v_a, pr, 0, 0, EXACT), 0.0)
        block = slice(128 * a, 128 * a + 128)
        mixT[block, block] = m_t.astype(BF)
        lhs_c[block, block] = m_t.T.astype(BF)

    def rear(i, _):
        s = pl.ds(pl.multiple_of(i * NB, NB), NB)
        sp = dg(mixT[...], wb[:, s], 1, 0).astype(BF)
        sT[:, s] = sp
        res = (pT[:, s].astype(F32) + dg(woT[...], sp, 1, 0)).astype(BF).astype(F32)
        xc = res - jnp.sum(res, axis=0, keepdims=True) * (1.0 / C)
        var = jnp.sum(xc * xc, axis=0, keepdims=True) * (1.0 / C)
        rstd = lax.rsqrt(var + EPS)
        xhat = xc * rstd
        xh2[...] = xhat
        n2 = (xhat * lanes4(g2c[...])).astype(BF)
        n2T[:, s] = n2
        for f in range(FF // 256):
            fr = slice(256 * f, 256 * f + 256)
            pre = dg(wuT[fr, :], n2, 1, 0)
            x2 = pre * pre
            h = 0.5 + 0.5 * jnp.tanh(pre * (K0 + K1 * x2))
            hT[fr, s] = (pre * h).astype(BF)
            slope = h + (pre * (2.0 * K0 + (6.0 * K1) * x2)) * (h - h * h)
            dpT[fr, s] = (dhT[fr, s] * slope).astype(BF)
        dy = dg(wu_v[...], dpT[:, s], 1, 0)
        xhat = xh2[...]
        ga2[...] += fold_lanes(dy * xhat)
        dx = dy * lanes4(g2c[...])
        m1 = jnp.sum(dx, axis=0, keepdims=True) * (1.0 / C)
        m2 = jnp.sum(dx * xhat, axis=0, keepdims=True) * (1.0 / C)
        dr = cT[:, s].astype(F32) + rstd * (dx - m1 - xhat * m2)
        drT[:, s] = dr
        low = dr.astype(BF)
        drb[:, s] = low
        dsT[:, s] = dg(wo_v[...], low, 1, 0).astype(BF)
        return 0

    lax.fori_loop(0, chunks, rear, 0)
    s2_src[0:64, :] = fold_diagonal(dg(wb[...], dsT[...], 1, 1))
    s2_src[64:72, :] = jnp.zeros((8, 128), F32)
    second = small_sum(net, s2_src, s2_core, s2_slots, s2_out)
    step_of(second)

    def put(left, right, at):
        v = dg(left, right, 1, 1)
        for j in range(v.shape[1] // 128):
            b_src[256 * (at + j) : 256 * (at + j + 1), :] = v[:, 128 * j : 128 * (j + 1)]

    bulk = bulk_sum(net, b_src, b_got0, b_sum0, b_got1, b_sum1, b_got2, b_slots, b_out)
    for f in range(4):
        fr = slice(256 * f, 256 * f + 256)
        put(n2T[...], dpT[fr, :], 2 * f)
        put(cT[...], hT[fr, :], 8 + 2 * f)
        if f == 3:
            put(sT[...], drb[...], 16)
        else:
            step_of(second)
    finish_of(second)
    step_of(bulk)

    dqs, dks, dvs = [], [], []
    for a in range(2):
        r = slice(32 * a, 32 * a + 32)
        q_a, k_a, v_a = qkv_s[r, 0:128], qkv_s[r, 128:256], qkv_s[r, 256:384]
        pr = prob_s[r, :]
        d_bd = tile_diagonal(s2_out[r, :])
        dvs.append(dg(pr, d_bd, 1, 0, EXACT))
        dp = dg(v_a, d_bd, 1, 1, EXACT)
        dsc = pr * (dp - jnp.sum(pr * dp, axis=0, keepdims=True)) * scale
        dq = jnp.where(mask4, dg(dsc, k_a, 0, 0, EXACT), 0.0)
        dqs.append(dq[0:32] + dq[32:64] + dq[64:96] + dq[96:128])
        dks.append(dg(dsc, tile_diagonal(q_a), 1, 0, EXACT))
    d_all = jnp.concatenate(
        [jnp.concatenate(v, axis=0) for v in (dqs, dks, dvs)], axis=1
    )
    d_tok = dg(d_all, bqkv[...], 1, 1, EXACT)
    tok = tok_s[...]
    d_num = d_tok / denb_s[...]
    d_den = -(d_num * tok)
    for a in range(2):
        r = slice(32 * a, 32 * a + 32)
        block = slice(128 * a, 128 * a + 128)
        bd = tile_diagonal(d_num[r])
        hi, lo = split2(bd)
        lhs_c[block, 256 + 128 * a : 384 + 128 * a] = hi
        lhs_c[block, 512 + 128 * a : 640 + 128 * a] = lo
        ddc[block, :] = jnp.broadcast_to(
            jnp.sum(tile_diagonal(d_den[r]), axis=1, keepdims=True), (128, 128)
        )
        hi_t, lo_t = split2(bd.T)
        dnT[block, :] = jnp.zeros((128, 512), BF)
        dnT[block, block] = hi_t
        dnT[block, 256 + 128 * a : 384 + 128 * a] = lo_t

    def finish(i):
        s = pl.ds(pl.multiple_of(i * NB, NB), NB)
        feats = mfT[256:512, s]
        dw = dg(lhs_c[...], jnp.concatenate([dsT[:, s], feats, feats], axis=0), 1, 0)
        sg, rt = sgs[:, s], rts[:, s]
        dts = []
        for h in range(HEADS):
            r = slice(32 * h, 32 * h + 32)
            w = ws[r, s]
            g = dw[r] + lanes4(ddc[r, :])
            d_l = w * (g - jnp.sum(w * g, axis=0, keepdims=True))
            inner = jnp.sum(d_l * ls[r, s], axis=0, keepdims=True)
            scale_h = rt[h : h + 1]
            dts.append(-(inner * scale_h) * sg[h : h + 1])
            hi, lo = split2(d_l * scale_h)
            dl_s[r, s] = hi
            dl_s[256 + 32 * h : 288 + 32 * h, s] = lo
        dt = jnp.concatenate(dts, axis=0)
        dt_hi = dt.astype(BF).astype(F32)
        dt_s[:, s] = jnp.concatenate([dt_hi, dt - dt_hi], axis=0).astype(BF)
        hi = dl_s[0:256, s]
        dm = dg(bdd[...], jnp.concatenate([hi, dl_s[256:512, s], hi], axis=0), 1, 0)
        for h in range(HEADS):
            r = slice(32 * h, 32 * h + 32)
            dmf_s[r, s] = (dm[r] + lanes4(wtc[r, :]) * dt[h : h + 1]).astype(BF)
        wbs = wb[:, s]
        dmf_s[256:512, s] = dg(dnT[...], jnp.concatenate([wbs, wbs], axis=0), 1, 0).astype(BF)
        dy = dg(wmf[...], dmf_s[:, s], 1, 0)
        rstd = stat[1:2, s]
        xhat = (pT[:, s].astype(F32) - stat[0:1, s]) * rstd
        ga1[...] += fold_lanes(dy * xhat)
        dx = dy * lanes4(g1c[...])
        m1 = jnp.sum(dx, axis=0, keepdims=True) * (1.0 / C)
        m2 = jnp.sum(dx * xhat, axis=0, keepdims=True) * (1.0 / C)
        out = (drT[:, s] + rstd * (dx - m1 - xhat * m2)).astype(BF)
        gp_v[s, :] = out.T

    for i in range(chunks):
        finish(i)
        step_of(bulk)
    stores = [pltpu.make_async_copy(gp_v, o_points, out_sems.at[0])]
    stores[0].start()

    gmf = dg(nT[...], dmf_s[...], 1, 1)
    for j in range(4):
        t_src[256 * j : 256 * (j + 1), :] = gmf[:, 128 * j : 128 * (j + 1)]
    mids = mfT[0:256, :]
    gs = dg(mids, dl_s[0:256, :], 1, 1) + dg(mids, dl_s[256:512, :], 1, 1)
    gs64 = fold_diagonal(gs)
    t_src[1024:1056, :] = gs64[0:32] + gs64[32:64]
    gt = dg(mids, dt_s[...], 1, 1)
    gt = jnp.where(iota((256, 16), 1) % 8 == iota((256, 16), 0) // 32, gt, 0.0)
    gt = jnp.sum(gt, axis=1, keepdims=True)
    gt32 = gt[0:32]
    for h in range(1, HEADS):
        gt32 = gt32 + gt[32 * h : 32 * h + 32]
    t_src[1056:1088, :] = jnp.broadcast_to(gt32, (32, 128))
    gain_rows = column_to_rows(jnp.sum(ga1[...], axis=1, keepdims=True)) + column_to_rows(
        jnp.sum(ga2[...], axis=1, keepdims=True)
    )
    t_src[1088:1096, :] = jnp.concatenate(gain_rows + [jnp.zeros((4, 128), F32)], axis=0)

    tail = tail_sum(net, t_src, t_got0, t_sum0, t_got1, t_slots1, t_slots2, t_out)
    step_of(tail)

    for i, (o, d) in enumerate(((o_q, dqs), (o_k, dks), (o_v, dvs))):
        full = jnp.where(mask4, dg(tok, jnp.concatenate(d, axis=0), 0, 0, EXACT), 0.0)
        o[...] = dg(dg(hot4, full, 0, 0, EXACT), hot4, 1, 0, EXACT)

    for _ in range(8):
        step_of(bulk)
        step_of(tail)

    def store_columns(src, at, out, count, sem):
        for j in range(count):
            copy = pltpu.make_async_copy(
                src.at[pl.ds(256 * (at + j), 256), :],
                out.at[:, pl.ds(128 * j, 128)],
                out_sems.at[sem + j],
            )
            copy.start()
            stores.append(copy)

    store_columns(b_out, 0, o_up, 8, 1)
    store_columns(b_out, 8, o_down, 8, 9)
    store_columns(b_out, 16, o_out, 2, 17)
    finish_of(tail)
    store_columns(t_out, 0, o_mid, 2, 19)
    store_columns(t_out, 2, o_feat, 2, 21)
    o_slice[...] = dg(t_out[1024:1056, :], hot4, 1, 0, EXACT)
    diag = iota((32, 128), 0) == iota((32, 128), 1)
    o_temp[...] = jnp.sum(jnp.where(diag, t_out[1056:1088, :], 0.0), axis=0, keepdims=True)[:, 0:32]
    o_one[:, 0:128] = t_out[1088:1089, :]
    o_one[:, 128:256] = t_out[1089:1090, :]
    o_two[:, 0:128] = t_out[1090:1091, :]
    o_two[:, 128:256] = t_out[1091:1092, :]
    for store in stores:
        store.wait()
    net.drain()


def call(active, n, args):
    (points, cotangent, gain_one, gain_two, w_mid, w_feat, w_out, w_up, w_down,
     w_slice, w_temp, w_q, w_k, w_v) = args
    vm = lambda *shape: pltpu.VMEM(shape, F32)
    vb = lambda *shape: pltpu.VMEM(shape, BF)
    any_spec = pl.BlockSpec(memory_space=pl.ANY)
    vmem_spec = pl.BlockSpec(memory_space=pltpu.VMEM)
    out_shape = (
        [jax.ShapeDtypeStruct((n, C), BF)]
        + [jax.ShapeDtypeStruct((C, C), F32)] * 3
        + [jax.ShapeDtypeStruct((C, FF), F32)] * 2
        + [jax.ShapeDtypeStruct((1, C), F32)] * 2
        + [jax.ShapeDtypeStruct((32, 32), F32), jax.ShapeDtypeStruct((1, 32), F32)]
        + [jax.ShapeDtypeStruct((32, 32), F32)] * 3
    )
    small = [vm(ROWS_S, 128), vm(ROWS_S, 128), vm(36 * PART_S, 128), vm(ROWS_S, 128)]
    scratch = (
        [vb(n, C), vb(n, C), vb(C, C), vb(C, C), vb(C, C), vb(C, FF), vb(C, FF)]
        + [vb(C, n), vb(C, n), vb(512, C), vb(C, 512), vb(C, C), vb(FF, C), vb(FF, C)]
        + [vm(C, 128), vm(C, 128), vm(C, 128), vb(800, C), vb(C, 768), vm(128, 384)]
        + [vm(8, n), vb(C, n), vb(512, n), vm(8, n), vm(8, n), vm(C, n), vm(C, n), vb(C, n), vm(C, 128)]
        + [vm(64, 128), vm(64, 384), vm(64, 128), vm(64, 128), vb(C, C), vb(C, 768), vb(C, 512), vm(C, 128)]
        + [vm(FF, n), vb(C, n), vb(C, n), vm(C, NB), vb(FF, n), vb(FF, n), vm(C, n), vb(C, n), vb(C, n),
           vm(C, 128), vm(C, 128)]
        + [vb(512, n), vb(16, n), vb(512, n), vb(n, C)]
        + small
        + small
        + [vm(ROWS_G, 128), vm(2304, 128), vm(2304, 128), vm(9 * 192, 128), vm(576, 128), vm(9 * 48, 128),
           vm(12 * 48, 128), vm(ROWS_G, 128)]
        + [vm(ROWS_T, 128), vm(576, 128), vm(576, 128), vm(9 * 48, 128), vm(12 * 48, 128), vm(12 * 48, 128),
           vm(ROWS_T, 128)]
        + [pltpu.SemaphoreType.DMA((7,)), pltpu.SemaphoreType.DMA((23,)),
           pltpu.SemaphoreType.DMA((160,)), pltpu.SemaphoreType.DMA((160,))]
    )

    def body(*refs):
        kernel(active, *refs)

    outs = pl.pallas_call(
        body,
        name="block_backward",
        out_shape=out_shape,
        in_specs=[any_spec] * 7 + [vmem_spec] * 7,
        out_specs=[any_spec] * 6 + [vmem_spec] * 7,
        scratch_shapes=scratch,
        compiler_params=pltpu.CompilerParams(
            vmem_limit_bytes=62 * 2**20,
            has_side_effects=True,
            **({"collective_id": 0} if active else {}),
        ),
    )(
        points, cotangent, w_mid, w_feat, w_out, w_up, w_down,
        gain_one.reshape(1, C), gain_two.reshape(1, C), w_slice, w_temp.reshape(1, 32), w_q, w_k, w_v,
    )
    outs = list(outs)
    outs[6], outs[7], outs[9] = outs[6].reshape(C), outs[7].reshape(C), outs[9].reshape(32)
    return tuple(outs)


def solution(mesh):
    rows_spec = P(("pts", "grp"), None)

    def local(*args):
        return call(True, args[0].shape[0], args)

    return jax.shard_map(
        local,
        mesh=mesh,
        in_specs=(rows_spec, rows_spec) + (P(),) * 12,
        out_specs=(rows_spec,) + (P(),) * 12,
        check_vma=False,
    )
```

```python
import jax
import jax.numpy as jnp
from jax import lax
from jax.experimental import pallas as pl
from jax.experimental.pallas import tpu as pltpu
from jax.sharding import PartitionSpec as P

F32 = jnp.float32
BF = jnp.bfloat16
MESH = pl.DeviceIdType.MESH
EXACT = lax.Precision.HIGHEST
C = 256
HEADS = 8
FF = 1024
NB = 1024
EPS = 1e-5
K0 = 0.7978845608028654
K1 = K0 * 0.044715
ROWS_S = 72
PART_S = 24
ROWS_G = 4608
ROWS_T = 1152


def dg(a, b, ca, cb, precision=None):
    return lax.dot_general(
        a, b, (((ca,), (cb,)), ((), ())), precision=precision, preferred_element_type=F32
    )


def split3(v):
    hi = v.astype(BF)
    rest = v - hi.astype(F32)
    mid = rest.astype(BF)
    low = (rest - mid.astype(F32)).astype(BF)
    return hi, mid, low


def split2(v):
    hi = v.astype(BF)
    return hi, (v - hi.astype(F32)).astype(BF)


def iota(shape, dim):
    return lax.broadcasted_iota(jnp.int32, shape, dim)


def same_block(rows, cols):
    return (iota((rows, cols), 0) // 32) == (iota((rows, cols), 1) // 32)


def one_hot_rows(rows):
    return ((iota((rows, 32), 0) % 32) == iota((rows, 32), 1)).astype(F32)


def lanes4(col):
    return jnp.concatenate([col] * (NB // 128), axis=1)


def fold_lanes(v):
    out = v[:, 0:128]
    for j in range(1, v.shape[1] // 128):
        out = out + v[:, 128 * j : 128 * (j + 1)]
    return out


def column_to_rows(col):
    eye = iota((128, 128), 0) == iota((128, 128), 1)
    rows = []
    for a in range(col.shape[0] // 128):
        spread = jnp.broadcast_to(col[128 * a : 128 * (a + 1)], (128, 128))
        rows.append(jnp.sum(jnp.where(eye, spread, 0.0), axis=0, keepdims=True))
    return rows


def fold_diagonal(full):
    parts = []
    mask = same_block(128, 128)
    for a in range(2):
        sub = jnp.where(mask, full[128 * a : 128 * (a + 1), 128 * a : 128 * (a + 1)], 0.0)
        parts.append(sub[0:32] + sub[32:64] + sub[64:96] + sub[96:128])
    return jnp.concatenate(parts, axis=0)


def tile_diagonal(compact):
    return jnp.where(same_block(128, 128), jnp.concatenate([compact] * 4, axis=0), 0.0)


class Net:
    def __init__(self, send_sems, recv_sems, active):
        self.send_sems, self.recv_sems, self.active = send_sems, recv_sems, active
        self.count, self.open = 0, []
        if active:
            pts, z = lax.axis_index("pts"), lax.axis_index("grp")
            core, y, x = pts % 2, (pts // 2) % 4, pts // 8
            self.core = core
            self.at = (x, y, z)
            self.partner = (pts + 1 - 2 * core, z)
            self.peer = (
                lambda j: (j * 8 + y * 2 + core, z),
                lambda j: (x * 8 + j * 2 + core, z),
                lambda j: (pts, j),
            )

    def hello(self):
        if not self.active:
            return
        barrier = pltpu.get_barrier_semaphore()
        pl.semaphore_signal(barrier, inc=1, device_id=self.partner, device_id_type=MESH)
        for ax in range(3):
            for d in range(1, 4):
                pl.semaphore_signal(
                    barrier,
                    inc=1,
                    device_id=self.peer[ax]((self.at[ax] + d) % 4),
                    device_id_type=MESH,
                )

    def ready(self):
        if self.active:
            pl.semaphore_wait(pltpu.get_barrier_semaphore(), 10)

    def send(self, src, dst, device):
        k = self.count
        self.count += 1
        copy = pltpu.make_async_remote_copy(
            src_ref=src,
            dst_ref=dst,
            send_sem=self.send_sems.at[k],
            recv_sem=self.recv_sems.at[k],
            device_id=device,
            device_id_type=MESH,
        )
        copy.start()
        self.open.append(copy)
        return copy

    def drain(self):
        for copy in self.open:
            copy.wait_send()
        self.open = []


def rows(start, size):
    return pl.ds(pl.multiple_of(start, 8), size)


def small_sum(net, src, from_core, slots, out):
    if not net.active:
        out[...] = src[...]
        return
    copy = net.send(src, from_core, net.partner)
    yield
    copy.wait_recv()
    parts = [
        src[PART_S * p : PART_S * (p + 1), :] + from_core[PART_S * p : PART_S * (p + 1), :]
        for p in range(3)
    ]
    for k in range(3):
        copies = []
        for p in range(3):
            ax = (p + k) % 3
            mine = rows(k * 12 * PART_S + (p * 4 + net.at[ax]) * PART_S, PART_S)
            slots[mine, :] = parts[p]
            for d in range(1, 4):
                copies.append(
                    net.send(slots.at[mine, :], slots.at[mine, :], net.peer[ax]((net.at[ax] + d) % 4))
                )
        yield
        for copy in copies:
            copy.wait_recv()
        for p in range(3):
            four = [
                slots[pl.ds(k * 12 * PART_S + (p * 4 + s) * PART_S, PART_S), :]
                for s in range(4)
            ]
            parts[p] = (four[0] + four[1]) + (four[2] + four[3])
    for p in range(3):
        out[PART_S * p : PART_S * (p + 1), :] = parts[p]


def core_scatter(net, src, got, summed, part, barrier_copies=None):
    half = part // 2
    copies = []
    for p in range(3):
        theirs = rows(p * part + (1 - net.core) * half, half)
        copies.append(net.send(src.at[theirs, :], got.at[pl.ds(p * half, half), :], net.partner))
    yield
    for p, copy in enumerate(copies):
        copy.wait_recv()
        here = pl.ds(p * half, half)
        summed[here, :] = src[rows(p * part + net.core * half, half), :] + got[here, :]


def axis_scatter(net, k, src, got, size, store):
    piece = size // 4
    copies = []
    for p in range(3):
        ax = (p + k) % 3
        for d in range(1, 4):
            j = (net.at[ax] + d) % 4
            copies.append(
                net.send(
                    src.at[rows(p * size + j * piece, piece), :],
                    got.at[pl.ds((p * 3 + d - 1) * piece, piece), :],
                    net.peer[ax](j),
                )
            )
    yield
    for copy in copies:
        copy.wait_recv()
    for p in range(3):
        ax = (p + k) % 3
        own = src[rows(p * size + net.at[ax] * piece, piece), :]
        three = [got[pl.ds((p * 3 + d) * piece, piece), :] for d in range(3)]
        store(p, (own + three[0]) + (three[1] + three[2]))


def axis_exchange(net, k, slots, size, store):
    copies = []
    for p in range(3):
        ax = (p + k) % 3
        mine = rows((p * 4 + net.at[ax]) * size, size)
        for d in range(1, 4):
            copies.append(
                net.send(slots.at[mine, :], slots.at[mine, :], net.peer[ax]((net.at[ax] + d) % 4))
            )
    yield
    for copy in copies:
        copy.wait_recv()
    for p in range(3):
        four = [slots[pl.ds((p * 4 + s) * size, size), :] for s in range(4)]
        store(p, (four[0] + four[1]) + (four[2] + four[3]))


def axis_gather(net, k, out, where):
    copies = []
    for p in range(3):
        ax = (p + k) % 3
        for d in range(1, 4):
            here = out.at[where(p), :]
            copies.append(net.send(here, here, net.peer[ax]((net.at[ax] + d) % 4)))
    yield
    for copy in copies:
        copy.wait_recv()


def core_gather(net, out, where):
    copies = [net.send(out.at[where(p), :], out.at[where(p), :], net.partner) for p in range(3)]
    yield
    for copy in copies:
        copy.wait_recv()


def bulk_sum(net, src, got0, sum0, got1, sum1, got2, slots, out):
    if not net.active:
        out[...] = src[...]
        return
    part, half, quarter, piece = 1536, 768, 192, 48
    yield from core_scatter(net, src, got0, sum0, part)

    def keep1(p, v):
        sum1[pl.ds(p * quarter, quarter), :] = v

    yield from axis_scatter(net, 0, sum0, got1, half, keep1)

    def keep2(p, v):
        slots[rows((p * 4 + net.at[(p + 2) % 3]) * piece, piece), :] = v

    yield from axis_scatter(net, 1, sum1, got2, quarter, keep2)

    def base(p, depth):
        at = p * part + net.core * half
        if depth > 0:
            at = at + net.at[p % 3] * quarter
        if depth > 1:
            at = at + net.at[(p + 1) % 3] * piece
        return at

    def keep3(p, v):
        out[rows(base(p, 2), piece), :] = v

    yield from axis_exchange(net, 2, slots, piece, keep3)
    yield from axis_gather(net, 1, out, lambda p: rows(base(p, 2), piece))
    yield from axis_gather(net, 0, out, lambda p: rows(base(p, 1), quarter))
    yield from core_gather(net, out, lambda p: rows(base(p, 0), half))


def tail_sum(net, src, got0, sum0, got1, slots1, slots2, out):
    if not net.active:
        out[...] = src[...]
        return
    part, half, piece = 384, 192, 48
    yield from core_scatter(net, src, got0, sum0, part)

    def keep(slots, k):
        def store(p, v):
            slots[rows((p * 4 + net.at[(p + k) % 3]) * piece, piece), :] = v

        return store

    yield from axis_scatter(net, 0, sum0, got1, half, keep(slots1, 1))
    yield from axis_exchange(net, 1, slots1, piece, keep(slots2, 2))

    def where(p, depth):
        at = p * part + net.core * half
        if depth > 0:
            at = at + net.at[p % 3] * piece
        return rows(at, piece if depth else half)

    def last(p, v):
        out[where(p, 1), :] = v

    yield from axis_exchange(net, 2, slots2, piece, last)
    yield from axis_gather(net, 0, out, lambda p: where(p, 1))
    yield from core_gather(net, out, lambda p: where(p, 0))


def step_of(gen):
    next(gen, None)


def finish_of(gen):
    for _ in gen:
        pass


def kernel(
    active,
    points_h, cot_h, w_mid_h, w_feat_h, w_out_h, w_up_h, w_down_h,
    gain_one, gain_two, w_slice, w_temp, w_q, w_k, w_v,
    gp_v, b_out, t_out, o_small,
    pts_v, cot_v, wm_v, wf_v, wo_v, wu_v, wd_v,
    pT, cT, wmfT, wmf, woT, wuT, wdT,
    g1c, g2c, wtc, bds, bdd, bqkv,
    stat, nT, mfT, rts, sgs, ls, ws, wb, dacc,
    tok_s, qkv_s, prob_s, denb_s, mixT, lhs_c, dnT, ddc,
    dhT, sT, n2T, xh2, hT, dpT, drT, drb, dsT, ga1, ga2,
    dl_s, dt_s, dmf_s,
    s1_src, s1_core, s1_slots, s1_out, s2_src, s2_core, s2_slots, s2_out,
    s3_src, s3_core, s3_slots, s3_out,
    b_src, b_got0, b_sum0, b_got1, b_sum1, b_got2, b_slots,
    t_src, t_got0, t_sum0, t_got1, t_slots1, t_slots2,
    in_sems, send_sems, recv_sems,
):
    n = pts_v.shape[0]
    chunks = n // NB
    net = Net(send_sems, recv_sems, active)
    net.hello()

    loads = [
        pltpu.make_async_copy(src, dst, in_sems.at[i])
        for i, (src, dst) in enumerate(
            [(w_mid_h, wm_v), (w_feat_h, wf_v), (points_h, pts_v), (cot_h, cot_v),
             (w_out_h, wo_v), (w_up_h, wu_v), (w_down_h, wd_v)]
        )
    ]
    for load in loads:
        load.start()

    hot = one_hot_rows(256)
    mask = same_block(256, 256)
    slice_t = jnp.where(mask, dg(dg(hot, w_slice[...], 1, 1, EXACT), hot, 1, 1, EXACT), 0.0)
    temp8 = jnp.where(
        iota((8, 256), 0) == iota((8, 256), 1) // 32,
        dg(jnp.broadcast_to(w_temp[...], (8, 32)), hot, 1, 1, EXACT),
        0.0,
    )
    for i, v in enumerate(split3(slice_t)):
        bds[256 * i : 256 * (i + 1), :] = v
    t_hi = temp8.astype(BF).astype(F32)
    t_mid = (temp8 - t_hi).astype(BF).astype(F32)
    t_low = temp8 - t_hi - t_mid
    bds[768:800, :] = jnp.concatenate([t_hi, t_mid, t_low, jnp.zeros((8, 256), F32)], axis=0).astype(BF)
    g1c[...] = jnp.broadcast_to(gain_one[...], (128, 256)).T
    dacc[...] = jnp.zeros_like(dacc)
    ga1[...] = jnp.zeros_like(ga1)
    ga2[...] = jnp.zeros_like(ga2)
    t_src[1024:ROWS_T, :] = jnp.zeros((ROWS_T - 1024, 128), F32)

    loads[0].wait()
    loads[1].wait()
    wmfT[0:256, :] = wm_v[...].T
    wmfT[256:512, :] = wf_v[...].T
    wmf[:, 0:256] = wm_v[...]
    wmf[:, 256:512] = wf_v[...]
    loads[2].wait()

    def front(i, _):
        s = pl.ds(pl.multiple_of(i * NB, NB), NB)
        xT = pts_v[s, :].T
        pT[:, s] = xT
        x = xT.astype(F32)
        mean = jnp.sum(x, axis=0, keepdims=True) * (1.0 / C)
        xc = x - mean
        var = jnp.sum(xc * xc, axis=0, keepdims=True) * (1.0 / C)
        rstd = lax.rsqrt(var + EPS)
        stat[0:1, s] = mean
        stat[1:2, s] = rstd
        normed = (xc * rstd * lanes4(g1c[...])).astype(BF)
        nT[:, s] = normed
        mf = dg(wmfT[...], normed, 1, 0).astype(BF)
        mfT[:, s] = mf
        lg = dg(bds[...], mf[0:256], 1, 0)
        t = lg[768:776] + lg[776:784] + lg[784:792]
        rt = 1.0 / (0.5 + (jnp.maximum(t, 0.0) + jnp.log(1.0 + jnp.exp(-jnp.abs(t)))))
        rts[:, s] = rt
        sgs[:, s] = 1.0 / (1.0 + jnp.exp(-t))
        for h in range(HEADS):
            r = slice(32 * h, 32 * h + 32)
            l = (lg[r] + lg[256 + 32 * h : 288 + 32 * h] + lg[512 + 32 * h : 544 + 32 * h]) * rt[h : h + 1]
            e = jnp.exp(l - jnp.max(l, axis=0, keepdims=True))
            w = e * (1.0 / jnp.sum(e, axis=0, keepdims=True))
            ls[r, s] = l
            ws[r, s] = w
            wb[r, s] = w.astype(BF)
            dacc[r, :] += fold_lanes(w)
        return 0

    for i in range(chunks):
        front(i, 0)
    s1_src[0:64, :] = fold_diagonal(dg(wb[...], mfT[256:512, :], 1, 1))
    den_rows = column_to_rows(jnp.sum(dacc[...], axis=1, keepdims=True))
    s1_src[64:72, :] = jnp.concatenate(den_rows + [jnp.zeros((6, 128), F32)], axis=0)

    net.ready()
    first = small_sum(net, s1_src, s1_core, s1_slots, s1_out)
    step_of(first)

    slice_n = jnp.where(mask, dg(dg(hot, w_slice[...], 1, 0, EXACT), hot, 1, 1, EXACT), 0.0)
    n_hi, n_lo = split2(slice_n)
    bdd[:, 0:256] = n_hi
    bdd[:, 256:512] = n_hi
    bdd[:, 512:768] = n_lo
    wtc[...] = dg(hot, jnp.broadcast_to(w_temp[...], (128, 32)), 1, 1, EXACT)
    g2c[...] = jnp.broadcast_to(gain_two[...], (128, 256)).T
    hot4 = one_hot_rows(128)
    mask4 = same_block(128, 128)
    for i, w in enumerate((w_q, w_k, w_v)):
        bqkv[:, 128 * i : 128 * (i + 1)] = jnp.where(
            mask4, dg(dg(hot4, w[...], 1, 0, EXACT), hot4, 1, 1, EXACT), 0.0
        )
    for i in range(3, 7):
        loads[i].wait()
    wdT[...] = wd_v[...].T

    def hidden_gradient(i):
        s = pl.ds(pl.multiple_of(i * NB, NB), NB)
        cT[:, s] = cot_v[s, :].T
        dhT[:, s] = dg(wdT[...], cT[:, s], 1, 0)

    hidden_gradient(0)
    step_of(first)
    for i in range(1, chunks):
        hidden_gradient(i)
    woT[...] = wo_v[...].T
    wuT[...] = wu_v[...].T
    finish_of(first)

    total = s1_out[0:64, :]
    picked = []
    pick = (iota((32, 128), 1) % 32) == iota((32, 128), 0)
    for a in range(2):
        picked.append(jnp.where(pick, jnp.broadcast_to(s1_out[64 + a : 65 + a, :], (32, 128)), 0.0))
    ones4 = mask4.astype(F32)
    denb = dg(jnp.concatenate(picked, axis=0), ones4, 1, 0, EXACT) + EPS
    denb_s[...] = denb
    tok = total / denb
    tok_s[...] = tok
    qkv = dg(tok, bqkv[...], 1, 0, EXACT)
    qkv_s[...] = qkv
    scale = 32.0 ** (-0.5)
    mixT[...] = jnp.zeros_like(mixT)
    lhs_c[...] = jnp.zeros_like(lhs_c)
    for a in range(2):
        r = slice(32 * a, 32 * a + 32)
        q_a, k_a, v_a = qkv[r, 0:128], qkv[r, 128:256], qkv[r, 256:384]
        sc = dg(k_a, tile_diagonal(q_a), 1, 1, EXACT) * scale
        e = jnp.exp(sc - jnp.max(sc, axis=0, keepdims=True))
        pr = e / jnp.sum(e, axis=0, keepdims=True)
        prob_s[r, :] = pr
        m_t = jnp.where(mask4, dg(v_a, pr, 0, 0, EXACT), 0.0)
        block = slice(128 * a, 128 * a + 128)
        mixT[block, block] = m_t.astype(BF)
        lhs_c[block, block] = m_t.T.astype(BF)

    def rear(i, _):
        s = pl.ds(pl.multiple_of(i * NB, NB), NB)
        sp = dg(mixT[...], wb[:, s], 1, 0).astype(BF)
        sT[:, s] = sp
        res = (pT[:, s].astype(F32) + dg(woT[...], sp, 1, 0)).astype(BF).astype(F32)
        xc = res - jnp.sum(res, axis=0, keepdims=True) * (1.0 / C)
        var = jnp.sum(xc * xc, axis=0, keepdims=True) * (1.0 / C)
        rstd = lax.rsqrt(var + EPS)
        xhat = xc * rstd
        xh2[...] = xhat
        n2 = (xhat * lanes4(g2c[...])).astype(BF)
        n2T[:, s] = n2
        for f in range(FF // 256):
            fr = slice(256 * f, 256 * f + 256)
            pre = dg(wuT[fr, :], n2, 1, 0)
            x2 = pre * pre
            h = 0.5 + 0.5 * jnp.tanh(pre * (K0 + K1 * x2))
            hT[fr, s] = (pre * h).astype(BF)
            slope = h + (pre * (2.0 * K0 + (6.0 * K1) * x2)) * (h - h * h)
            dpT[fr, s] = (dhT[fr, s] * slope).astype(BF)
        dy = dg(wu_v[...], dpT[:, s], 1, 0)
        xhat = xh2[...]
        ga2[...] += fold_lanes(dy * xhat)
        dx = dy * lanes4(g2c[...])
        m1 = jnp.sum(dx, axis=0, keepdims=True) * (1.0 / C)
        m2 = jnp.sum(dx * xhat, axis=0, keepdims=True) * (1.0 / C)
        dr = cT[:, s].astype(F32) + rstd * (dx - m1 - xhat * m2)
        drT[:, s] = dr
        low = dr.astype(BF)
        drb[:, s] = low
        dsT[:, s] = dg(wo_v[...], low, 1, 0).astype(BF)
        return 0

    for i in range(chunks):
        rear(i, 0)
    s2_src[0:64, :] = fold_diagonal(dg(wb[...], dsT[...], 1, 1))
    s2_src[64:72, :] = jnp.zeros((8, 128), F32)
    second = small_sum(net, s2_src, s2_core, s2_slots, s2_out)
    step_of(second)

    def put(left, right, at):
        v = dg(left, right, 1, 1)
        for j in range(v.shape[1] // 128):
            b_src[256 * (at + j) : 256 * (at + j + 1), :] = v[:, 128 * j : 128 * (j + 1)]

    bulk = bulk_sum(net, b_src, b_got0, b_sum0, b_got1, b_sum1, b_got2, b_slots, b_out)
    for f in range(4):
        fr = slice(256 * f, 256 * f + 256)
        put(n2T[...], dpT[fr, :], 2 * f)
        put(cT[...], hT[fr, :], 8 + 2 * f)
        if f == 1:
            step_of(second)
    put(sT[...], drb[...], 16)
    step_of(bulk)
    step_of(second)
    step_of(bulk)
    step_of(second)
    finish_of(second)

    dqs, dks, dvs = [], [], []
    for a in range(2):
        r = slice(32 * a, 32 * a + 32)
        q_a, k_a, v_a = qkv_s[r, 0:128], qkv_s[r, 128:256], qkv_s[r, 256:384]
        pr = prob_s[r, :]
        d_bd = tile_diagonal(s2_out[r, :])
        dvs.append(dg(pr, d_bd, 1, 0, EXACT))
        dp = dg(v_a, d_bd, 1, 1, EXACT)
        dsc = pr * (dp - jnp.sum(pr * dp, axis=0, keepdims=True)) * scale
        dq = jnp.where(mask4, dg(dsc, k_a, 0, 0, EXACT), 0.0)
        dqs.append(dq[0:32] + dq[32:64] + dq[64:96] + dq[96:128])
        dks.append(dg(dsc, tile_diagonal(q_a), 1, 0, EXACT))
    d_all = jnp.concatenate(
        [jnp.concatenate(v, axis=0) for v in (dqs, dks, dvs)], axis=1
    )
    d_tok = dg(d_all, bqkv[...], 1, 1, EXACT)
    tok = tok_s[...]
    d_num = d_tok / denb_s[...]
    d_den = -(d_num * tok)
    for a in range(2):
        r = slice(32 * a, 32 * a + 32)
        block = slice(128 * a, 128 * a + 128)
        bd = tile_diagonal(d_num[r])
        hi, lo = split2(bd)
        lhs_c[block, 256 + 128 * a : 384 + 128 * a] = hi
        lhs_c[block, 512 + 128 * a : 640 + 128 * a] = lo
        ddc[block, :] = jnp.broadcast_to(
            jnp.sum(tile_diagonal(d_den[r]), axis=1, keepdims=True), (128, 128)
        )
        hi_t, lo_t = split2(bd.T)
        dnT[block, :] = jnp.zeros((128, 512), BF)
        dnT[block, block] = hi_t
        dnT[block, 256 + 128 * a : 384 + 128 * a] = lo_t

    def finish(i):
        s = pl.ds(pl.multiple_of(i * NB, NB), NB)
        feats = mfT[256:512, s]
        dw = dg(lhs_c[...], jnp.concatenate([dsT[:, s], feats, feats], axis=0), 1, 0)
        sg, rt = sgs[:, s], rts[:, s]
        dts = []
        for h in range(HEADS):
            r = slice(32 * h, 32 * h + 32)
            w = ws[r, s]
            g = dw[r] + lanes4(ddc[r, :])
            d_l = w * (g - jnp.sum(w * g, axis=0, keepdims=True))
            inner = jnp.sum(d_l * ls[r, s], axis=0, keepdims=True)
            scale_h = rt[h : h + 1]
            dts.append(-(inner * scale_h) * sg[h : h + 1])
            hi, lo = split2(d_l * scale_h)
            dl_s[r, s] = hi
            dl_s[256 + 32 * h : 288 + 32 * h, s] = lo
        dt = jnp.concatenate(dts, axis=0)
        dt_hi = dt.astype(BF).astype(F32)
        dt_s[:, s] = jnp.concatenate([dt_hi, dt - dt_hi], axis=0).astype(BF)
        hi = dl_s[0:256, s]
        dm = dg(bdd[...], jnp.concatenate([hi, dl_s[256:512, s], hi], axis=0), 1, 0)
        for h in range(HEADS):
            r = slice(32 * h, 32 * h + 32)
            dmf_s[r, s] = (dm[r] + lanes4(wtc[r, :]) * dt[h : h + 1]).astype(BF)
        wbs = wb[:, s]
        dmf_s[256:512, s] = dg(dnT[...], jnp.concatenate([wbs, wbs], axis=0), 1, 0).astype(BF)

    def points_gradient(i):
        s = pl.ds(pl.multiple_of(i * NB, NB), NB)
        dy = dg(wmf[...], dmf_s[:, s], 1, 0)
        rstd = stat[1:2, s]
        xhat = (pT[:, s].astype(F32) - stat[0:1, s]) * rstd
        ga1[...] += fold_lanes(dy * xhat)
        dx = dy * lanes4(g1c[...])
        m1 = jnp.sum(dx, axis=0, keepdims=True) * (1.0 / C)
        m2 = jnp.sum(dx * xhat, axis=0, keepdims=True) * (1.0 / C)
        out = (drT[:, s] + rstd * (dx - m1 - xhat * m2)).astype(BF)
        gp_v[s, :] = out.T

    for i in range(chunks):
        finish(i)
        step_of(bulk)

    gmf = dg(nT[...], dmf_s[...], 1, 1)
    for j in range(4):
        t_src[256 * j : 256 * (j + 1), :] = gmf[:, 128 * j : 128 * (j + 1)]
    mids = mfT[0:256, :]
    gs = dg(mids, dl_s[0:256, :], 1, 1) + dg(mids, dl_s[256:512, :], 1, 1)
    gs64 = fold_diagonal(gs)
    t_src[1024:1056, :] = gs64[0:32] + gs64[32:64]
    gt = dg(mids, dt_s[...], 1, 1)
    gt = jnp.where(iota((256, 16), 1) % 8 == iota((256, 16), 0) // 32, gt, 0.0)
    gt = jnp.sum(gt, axis=1, keepdims=True)
    gt32 = gt[0:32]
    for h in range(1, HEADS):
        gt32 = gt32 + gt[32 * h : 32 * h + 32]
    t_src[1056:1088, :] = jnp.broadcast_to(gt32, (32, 128))
    tail = tail_sum(net, t_src, t_got0, t_sum0, t_got1, t_slots1, t_slots2, t_out)
    step_of(tail)
    points_gradient(0)
    step_of(tail)
    for i in range(1, chunks):
        points_gradient(i)
    gain_rows = column_to_rows(jnp.sum(ga1[...], axis=1, keepdims=True)) + column_to_rows(
        jnp.sum(ga2[...], axis=1, keepdims=True)
    )
    s3_src[0:8, :] = jnp.concatenate(gain_rows + [jnp.zeros((4, 128), F32)], axis=0)
    s3_src[8:ROWS_S, :] = jnp.zeros((ROWS_S - 8, 128), F32)
    third = small_sum(net, s3_src, s3_core, s3_slots, s3_out)
    step_of(third)
    step_of(bulk)
    step_of(third)

    for i, d in enumerate((dqs, dks, dvs)):
        full = jnp.where(mask4, dg(tok, jnp.concatenate(d, axis=0), 0, 0, EXACT), 0.0)
        o_small[32 * i : 32 * (i + 1), :] = dg(hot4, full, 0, 0, EXACT)

    for _ in range(8):
        step_of(tail)
        step_of(bulk)
        step_of(third)
    o_small[96:104, :] = s3_out[0:8, :]
    o_small[104:168, :] = t_out[1024:1088, :]
    net.drain()


def unpack(
    gp, bulk, tail, small,
    o_points, o_mid, o_feat, o_out, o_up, o_down,
    o_one, o_two, o_slice, o_temp, o_q, o_k, o_v,
    sems,
):
    stores = [pltpu.make_async_copy(gp, o_points, sems.at[0])]
    stores[0].start()

    def store_columns(src, at, out, count, sem):
        for j in range(count):
            copy = pltpu.make_async_copy(
                src.at[pl.ds(256 * (at + j), 256), :],
                out.at[:, pl.ds(128 * j, 128)],
                sems.at[sem + j],
            )
            copy.start()
            stores.append(copy)

    store_columns(bulk, 0, o_up, 8, 1)
    store_columns(bulk, 8, o_down, 8, 9)
    store_columns(bulk, 16, o_out, 2, 17)
    store_columns(tail, 0, o_mid, 2, 19)
    store_columns(tail, 2, o_feat, 2, 21)
    hot4 = one_hot_rows(128)
    for i, o in enumerate((o_q, o_k, o_v)):
        o[...] = dg(small[32 * i : 32 * (i + 1), :], hot4, 1, 0, EXACT)
    o_slice[...] = dg(small[104:136, :], hot4, 1, 0, EXACT)
    diag = iota((32, 128), 0) == iota((32, 128), 1)
    o_temp[...] = jnp.sum(jnp.where(diag, small[136:168, :], 0.0), axis=0, keepdims=True)[:, 0:32]
    o_one[:, 0:128] = small[96:97, :]
    o_one[:, 128:256] = small[97:98, :]
    o_two[:, 0:128] = small[98:99, :]
    o_two[:, 128:256] = small[99:100, :]
    for store in stores:
        store.wait()


def call(active, n, args):
    (points, cotangent, gain_one, gain_two, w_mid, w_feat, w_out, w_up, w_down,
     w_slice, w_temp, w_q, w_k, w_v) = args
    vm = lambda *shape: pltpu.VMEM(shape, F32)
    vb = lambda *shape: pltpu.VMEM(shape, BF)
    any_spec = pl.BlockSpec(memory_space=pl.ANY)
    vmem_spec = pl.BlockSpec(memory_space=pltpu.VMEM)
    out_shape = (
        [jax.ShapeDtypeStruct((n, C), BF)]
        + [jax.ShapeDtypeStruct((C, C), F32)] * 3
        + [jax.ShapeDtypeStruct((C, FF), F32)] * 2
        + [jax.ShapeDtypeStruct((1, C), F32)] * 2
        + [jax.ShapeDtypeStruct((32, 32), F32), jax.ShapeDtypeStruct((1, 32), F32)]
        + [jax.ShapeDtypeStruct((32, 32), F32)] * 3
    )
    small = [vm(ROWS_S, 128), vm(ROWS_S, 128), vm(36 * PART_S, 128), vm(ROWS_S, 128)]
    scratch = (
        [vb(n, C), vb(n, C), vb(C, C), vb(C, C), vb(C, C), vb(C, FF), vb(C, FF)]
        + [vb(C, n), vb(C, n), vb(512, C), vb(C, 512), vb(C, C), vb(FF, C), vb(FF, C)]
        + [vm(C, 128), vm(C, 128), vm(C, 128), vb(800, C), vb(C, 768), vm(128, 384)]
        + [vm(8, n), vb(C, n), vb(512, n), vm(8, n), vm(8, n), vm(C, n), vm(C, n), vb(C, n), vm(C, 128)]
        + [vm(64, 128), vm(64, 384), vm(64, 128), vm(64, 128), vb(C, C), vb(C, 768), vb(C, 512), vm(C, 128)]
        + [vm(FF, n), vb(C, n), vb(C, n), vm(C, NB), vb(FF, n), vb(FF, n), vm(C, n), vb(C, n), vb(C, n),
           vm(C, 128), vm(C, 128)]
        + [vb(512, n), vb(16, n), vb(512, n)]
        + small
        + small
        + small
        + [vm(ROWS_G, 128), vm(2304, 128), vm(2304, 128), vm(9 * 192, 128), vm(576, 128), vm(9 * 48, 128),
           vm(12 * 48, 128)]
        + [vm(ROWS_T, 128), vm(576, 128), vm(576, 128), vm(9 * 48, 128), vm(12 * 48, 128), vm(12 * 48, 128)]
        + [pltpu.SemaphoreType.DMA((7,)),
           pltpu.SemaphoreType.DMA((192,)), pltpu.SemaphoreType.DMA((192,))]
    )

    def body(*refs):
        kernel(active, *refs)

    mid_shape = [pltpu.VMEM((n, C), BF), pltpu.VMEM((ROWS_G, 128), F32), pltpu.VMEM((ROWS_T, 128), F32),
                 pltpu.VMEM((168, 128), F32)]
    packed = pl.pallas_call(
        body,
        name="block_backward",
        out_shape=mid_shape,
        in_specs=[any_spec] * 7 + [vmem_spec] * 7,
        out_specs=[vmem_spec] * 4,
        scratch_shapes=scratch,
        compiler_params=pltpu.CompilerParams(
            vmem_limit_bytes=56 * 2**20,
            has_side_effects=True,
            **({"collective_id": 0} if active else {}),
        ),
    )(
        points, cotangent, w_mid, w_feat, w_out, w_up, w_down,
        gain_one.reshape(1, C), gain_two.reshape(1, C), w_slice, w_temp.reshape(1, 32), w_q, w_k, w_v,
    )
    outs = pl.pallas_call(
        unpack,
        name="unpack",
        out_shape=out_shape,
        in_specs=[vmem_spec] * 4,
        out_specs=[any_spec] * 6 + [vmem_spec] * 7,
        scratch_shapes=[pltpu.SemaphoreType.DMA((23,))],
        compiler_params=pltpu.CompilerParams(vmem_limit_bytes=4 * 2**20),
    )(*packed)
    outs = list(outs)
    outs[6], outs[7], outs[9] = outs[6].reshape(C), outs[7].reshape(C), outs[9].reshape(32)
    return tuple(outs)


def solution(mesh):
    rows_spec = P(("pts", "grp"), None)

    def local(*args):
        return call(True, args[0].shape[0], args)

    return jax.shard_map(
        local,
        mesh=mesh,
        in_specs=(rows_spec, rows_spec) + (P(),) * 12,
        out_specs=(rows_spec,) + (P(),) * 12,
        check_vma=False,
    )
```

```python
import jax
import jax.numpy as jnp
from jax import lax
from jax.experimental import pallas as pl
from jax.experimental.pallas import tpu as pltpu
from jax.sharding import PartitionSpec as P

F32 = jnp.float32
BF = jnp.bfloat16
MESH = pl.DeviceIdType.MESH
EXACT = lax.Precision.HIGHEST
C = 256
HEADS = 8
FF = 1024
NB = 1024
EPS = 1e-5
K0 = 0.7978845608028654
K1 = K0 * 0.044715
ROWS_S = 72
PART_S = 24
ROWS_G = 4608
ROWS_T = 1152


def dg(a, b, ca, cb, precision=None):
    return lax.dot_general(
        a, b, (((ca,), (cb,)), ((), ())), precision=precision, preferred_element_type=F32
    )


def split3(v):
    hi = v.astype(BF)
    rest = v - hi.astype(F32)
    mid = rest.astype(BF)
    low = (rest - mid.astype(F32)).astype(BF)
    return hi, mid, low


def split2(v):
    hi = v.astype(BF)
    return hi, (v - hi.astype(F32)).astype(BF)


def iota(shape, dim):
    return lax.broadcasted_iota(jnp.int32, shape, dim)


def same_block(rows, cols):
    return (iota((rows, cols), 0) // 32) == (iota((rows, cols), 1) // 32)


def one_hot_rows(rows):
    return ((iota((rows, 32), 0) % 32) == iota((rows, 32), 1)).astype(F32)


def lanes4(col):
    return jnp.concatenate([col] * (NB // 128), axis=1)


def fold_lanes(v):
    out = v[:, 0:128]
    for j in range(1, v.shape[1] // 128):
        out = out + v[:, 128 * j : 128 * (j + 1)]
    return out


def column_to_rows(col):
    eye = iota((128, 128), 0) == iota((128, 128), 1)
    rows = []
    for a in range(col.shape[0] // 128):
        spread = jnp.broadcast_to(col[128 * a : 128 * (a + 1)], (128, 128))
        rows.append(jnp.sum(jnp.where(eye, spread, 0.0), axis=0, keepdims=True))
    return rows


def fold_diagonal(full):
    parts = []
    mask = same_block(128, 128)
    for a in range(2):
        sub = jnp.where(mask, full[128 * a : 128 * (a + 1), 128 * a : 128 * (a + 1)], 0.0)
        parts.append(sub[0:32] + sub[32:64] + sub[64:96] + sub[96:128])
    return jnp.concatenate(parts, axis=0)


def tile_diagonal(compact):
    return jnp.where(same_block(128, 128), jnp.concatenate([compact] * 4, axis=0), 0.0)


class Net:
    def __init__(self, send_sems, recv_sems, active):
        self.send_sems, self.recv_sems, self.active = send_sems, recv_sems, active
        self.count, self.open = 0, []
        if active:
            pts, z = lax.axis_index("pts"), lax.axis_index("grp")
            core, y, x = pts % 2, (pts // 2) % 4, pts // 8
            self.core = core
            self.at = (x, y, z)
            self.partner = (pts + 1 - 2 * core, z)
            other = 1 - core
            self.peer = (
                lambda j: (j * 8 + y * 2 + core, z),
                lambda j: (x * 8 + j * 2 + core, z),
                lambda j: (pts, j),
            )
            self.cross = (
                lambda j: (j * 8 + y * 2 + other, z),
                lambda j: (x * 8 + j * 2 + other, z),
                lambda j: (x * 8 + y * 2 + other, j),
            )

    def eight(self, ax):
        out = []
        for d in range(4):
            j = (self.at[ax] + d) % 4
            if d > 0:
                out.append((2 * d, j, self.core, self.peer[ax](j)))
            out.append((2 * d + 1, j, 1 - self.core, self.cross[ax](j)))
        return out

    def hello(self):
        if not self.active:
            return
        barrier = pltpu.get_barrier_semaphore()
        devices = [self.partner]
        for ax in range(3):
            for d in range(1, 4):
                j = (self.at[ax] + d) % 4
                devices += [self.peer[ax](j), self.cross[ax](j)]
        for device in devices:
            pl.semaphore_signal(barrier, inc=1, device_id=device, device_id_type=MESH)

    def ready(self):
        if self.active:
            pl.semaphore_wait(pltpu.get_barrier_semaphore(), 19)

    def send(self, src, dst, device):
        k = self.count
        self.count += 1
        copy = pltpu.make_async_remote_copy(
            src_ref=src,
            dst_ref=dst,
            send_sem=self.send_sems.at[k],
            recv_sem=self.recv_sems.at[k],
            device_id=device,
            device_id_type=MESH,
        )
        copy.start()
        self.open.append(copy)
        return copy

    def drain(self):
        for copy in self.open:
            copy.wait_send()
        self.open = []


def rows(start, size):
    return pl.ds(pl.multiple_of(start, 8), size)


def add_all(v):
    while len(v) > 1:
        v = [v[k] + v[k + 1] for k in range(0, len(v), 2)]
    return v[0]


def small_sum(net, src, slots, out):
    if not net.active:
        out[...] = src[...]
        return
    parts = [src[PART_S * p : PART_S * (p + 1), :] for p in range(3)]
    base = 0
    for k in range(3):
        wide = 8 if k == 0 else 4
        copies = []
        for p in range(3):
            ax = (p + k) % 3
            here = 2 * net.at[ax] + net.core if k == 0 else net.at[ax]
            mine = rows(base + (p * wide + here) * PART_S, PART_S)
            slots[mine, :] = parts[p]
            devices = [item[3] for item in net.eight(ax)]
            if k > 0:
                devices = [net.peer[ax]((net.at[ax] + d) % 4) for d in range(1, 4)]
            for device in devices:
                copies.append(net.send(slots.at[mine, :], slots.at[mine, :], device))
        yield
        for copy in copies:
            copy.wait_recv()
        for p in range(3):
            parts[p] = add_all(
                [slots[pl.ds(base + (p * wide + t) * PART_S, PART_S), :] for t in range(wide)]
            )
        base += 3 * wide * PART_S
    for p in range(3):
        out[PART_S * p : PART_S * (p + 1), :] = parts[p]


def core_scatter(net, src, got, summed, part, barrier_copies=None):
    half = part // 2
    copies = []
    for p in range(3):
        theirs = rows(p * part + (1 - net.core) * half, half)
        copies.append(net.send(src.at[theirs, :], got.at[pl.ds(p * half, half), :], net.partner))
    yield
    for p, copy in enumerate(copies):
        copy.wait_recv()
        here = pl.ds(p * half, half)
        summed[here, :] = src[rows(p * part + net.core * half, half), :] + got[here, :]


def axis_scatter(net, k, src, got, size, store):
    piece = size // 4
    copies = []
    for p in range(3):
        ax = (p + k) % 3
        for d in range(1, 4):
            j = (net.at[ax] + d) % 4
            copies.append(
                net.send(
                    src.at[rows(p * size + j * piece, piece), :],
                    got.at[pl.ds((p * 3 + d - 1) * piece, piece), :],
                    net.peer[ax](j),
                )
            )
    yield
    for copy in copies:
        copy.wait_recv()
    for p in range(3):
        ax = (p + k) % 3
        own = src[rows(p * size + net.at[ax] * piece, piece), :]
        three = [got[pl.ds((p * 3 + d) * piece, piece), :] for d in range(3)]
        store(p, (own + three[0]) + (three[1] + three[2]))


def axis_exchange(net, k, slots, size, store):
    copies = []
    for p in range(3):
        ax = (p + k) % 3
        mine = rows((p * 4 + net.at[ax]) * size, size)
        for d in range(1, 4):
            copies.append(
                net.send(slots.at[mine, :], slots.at[mine, :], net.peer[ax]((net.at[ax] + d) % 4))
            )
    yield
    for copy in copies:
        copy.wait_recv()
    for p in range(3):
        four = [slots[pl.ds((p * 4 + s) * size, size), :] for s in range(4)]
        store(p, (four[0] + four[1]) + (four[2] + four[3]))


def axis_gather(net, k, out, where):
    copies = []
    for p in range(3):
        ax = (p + k) % 3
        for d in range(1, 4):
            here = out.at[where(p), :]
            copies.append(net.send(here, here, net.peer[ax]((net.at[ax] + d) % 4)))
    yield
    for copy in copies:
        copy.wait_recv()


def core_gather(net, out, where):
    copies = [net.send(out.at[where(p), :], out.at[where(p), :], net.partner) for p in range(3)]
    yield
    for copy in copies:
        copy.wait_recv()


def bulk_sum(net, src, got0, sum0, got1, sum1, got2, slots, out):
    if not net.active:
        out[...] = src[...]
        return
    part, half, quarter, piece = 1536, 768, 192, 48
    yield from core_scatter(net, src, got0, sum0, part)

    def keep1(p, v):
        sum1[pl.ds(p * quarter, quarter), :] = v

    yield from axis_scatter(net, 0, sum0, got1, half, keep1)

    def keep2(p, v):
        slots[rows((p * 4 + net.at[(p + 2) % 3]) * piece, piece), :] = v

    yield from axis_scatter(net, 1, sum1, got2, quarter, keep2)

    def base(p, depth):
        at = p * part + net.core * half
        if depth > 0:
            at = at + net.at[p % 3] * quarter
        if depth > 1:
            at = at + net.at[(p + 1) % 3] * piece
        return at

    def keep3(p, v):
        out[rows(base(p, 2), piece), :] = v

    yield from axis_exchange(net, 2, slots, piece, keep3)
    yield from axis_gather(net, 1, out, lambda p: rows(base(p, 2), piece))
    yield from axis_gather(net, 0, out, lambda p: rows(base(p, 1), quarter))
    yield from core_gather(net, out, lambda p: rows(base(p, 0), half))


def tail_sum(net, src, got, slots1, slots2, out):
    if not net.active:
        out[...] = src[...]
        return
    part, piece = 384, 48

    def where(p, j, core):
        return rows(p * part + (2 * j + core) * piece, piece)

    copies = []
    for p in range(3):
        for t, j, core, device in net.eight(p):
            there = got.at[pl.ds((p * 8 + t) * piece, piece), :]
            copies.append(net.send(src.at[where(p, j, core), :], there, device))
    yield
    for copy in copies:
        copy.wait_recv()
    for p in range(3):
        terms = [src[where(p, net.at[p], net.core), :]]
        terms += [got[pl.ds((p * 8 + t) * piece, piece), :] for t in range(1, 8)]
        slots1[rows((p * 4 + net.at[(p + 1) % 3]) * piece, piece), :] = add_all(terms)

    def keep(p, v):
        slots2[rows((p * 4 + net.at[(p + 2) % 3]) * piece, piece), :] = v

    yield from axis_exchange(net, 1, slots1, piece, keep)

    def last(p, v):
        out[where(p, net.at[p], net.core), :] = v

    yield from axis_exchange(net, 2, slots2, piece, last)
    copies = []
    for p in range(3):
        here = out.at[where(p, net.at[p], net.core), :]
        copies += [net.send(here, here, item[3]) for item in net.eight(p)]
    yield
    for copy in copies:
        copy.wait_recv()


def step_of(gen):
    next(gen, None)


def finish_of(gen):
    for _ in gen:
        pass


def kernel(
    active,
    points_h, cot_h, w_mid_h, w_feat_h, w_out_h, w_up_h, w_down_h,
    gain_one, gain_two, w_slice, w_temp, w_q, w_k, w_v,
    gp_v, b_out, t_out, o_small,
    pts_v, cot_v, wm_v, wf_v, wo_v, wu_v, wd_v,
    pT, cT, wmfT, wmf, woT, wuT, wdT,
    g1c, g2c, wtc, bds, bdd, bqkv,
    stat, nT, mfT, rts, sgs, ls, ws, wb, dacc,
    tok_s, qkv_s, prob_s, denb_s, mixT, lhs_c, dnT, ddc,
    dhT, sT, n2T, xh2, hT, dpT, drT, drb, dsT, ga1, ga2,
    dl_s, dt_s, dmf_s,
    s1_src, s1_slots, s1_out, s2_src, s2_slots, s2_out,
    s3_src, s3_slots, s3_out,
    b_src, b_got0, b_sum0, b_got1, b_sum1, b_got2, b_slots,
    t_src, t_got, t_slots1, t_slots2,
    in_sems, send_sems, recv_sems,
):
    n = pts_v.shape[0]
    chunks = n // NB
    net = Net(send_sems, recv_sems, active)
    net.hello()

    loads = [
        pltpu.make_async_copy(src, dst, in_sems.at[i])
        for i, (src, dst) in enumerate(
            [(w_mid_h, wm_v), (w_feat_h, wf_v), (points_h, pts_v), (cot_h, cot_v),
             (w_out_h, wo_v), (w_up_h, wu_v), (w_down_h, wd_v)]
        )
    ]
    for load in loads:
        load.start()

    hot = one_hot_rows(256)
    mask = same_block(256, 256)
    slice_t = jnp.where(mask, dg(dg(hot, w_slice[...], 1, 1, EXACT), hot, 1, 1, EXACT), 0.0)
    temp8 = jnp.where(
        iota((8, 256), 0) == iota((8, 256), 1) // 32,
        dg(jnp.broadcast_to(w_temp[...], (8, 32)), hot, 1, 1, EXACT),
        0.0,
    )
    for i, v in enumerate(split3(slice_t)):
        bds[256 * i : 256 * (i + 1), :] = v
    t_hi = temp8.astype(BF).astype(F32)
    t_mid = (temp8 - t_hi).astype(BF).astype(F32)
    t_low = temp8 - t_hi - t_mid
    bds[768:800, :] = jnp.concatenate([t_hi, t_mid, t_low, jnp.zeros((8, 256), F32)], axis=0).astype(BF)
    g1c[...] = jnp.broadcast_to(gain_one[...], (128, 256)).T
    dacc[...] = jnp.zeros_like(dacc)
    ga1[...] = jnp.zeros_like(ga1)
    ga2[...] = jnp.zeros_like(ga2)
    t_src[1024:ROWS_T, :] = jnp.zeros((ROWS_T - 1024, 128), F32)

    loads[0].wait()
    loads[1].wait()
    wmfT[0:256, :] = wm_v[...].T
    wmfT[256:512, :] = wf_v[...].T
    wmf[:, 0:256] = wm_v[...]
    wmf[:, 256:512] = wf_v[...]
    loads[2].wait()

    def front(i, _):
        s = pl.ds(pl.multiple_of(i * NB, NB), NB)
        xT = pts_v[s, :].T
        pT[:, s] = xT
        x = xT.astype(F32)
        mean = jnp.sum(x, axis=0, keepdims=True) * (1.0 / C)
        xc = x - mean
        var = jnp.sum(xc * xc, axis=0, keepdims=True) * (1.0 / C)
        rstd = lax.rsqrt(var + EPS)
        stat[0:1, s] = mean
        stat[1:2, s] = rstd
        normed = (xc * rstd * lanes4(g1c[...])).astype(BF)
        nT[:, s] = normed
        mf = dg(wmfT[...], normed, 1, 0).astype(BF)
        mfT[:, s] = mf
        lg = dg(bds[...], mf[0:256], 1, 0)
        t = lg[768:776] + lg[776:784] + lg[784:792]
        rt = 1.0 / (0.5 + (jnp.maximum(t, 0.0) + jnp.log(1.0 + jnp.exp(-jnp.abs(t)))))
        rts[:, s] = rt
        sgs[:, s] = 1.0 / (1.0 + jnp.exp(-t))
        for h in range(HEADS):
            r = slice(32 * h, 32 * h + 32)
            l = (lg[r] + lg[256 + 32 * h : 288 + 32 * h] + lg[512 + 32 * h : 544 + 32 * h]) * rt[h : h + 1]
            e = jnp.exp(l - jnp.max(l, axis=0, keepdims=True))
            w = e * (1.0 / jnp.sum(e, axis=0, keepdims=True))
            ls[r, s] = l
            ws[r, s] = w
            wb[r, s] = w.astype(BF)
            dacc[r, :] += fold_lanes(w)
        return 0

    for i in range(chunks):
        front(i, 0)
    s1_src[0:64, :] = fold_diagonal(dg(wb[...], mfT[256:512, :], 1, 1))
    den_rows = column_to_rows(jnp.sum(dacc[...], axis=1, keepdims=True))
    s1_src[64:72, :] = jnp.concatenate(den_rows + [jnp.zeros((6, 128), F32)], axis=0)

    net.ready()
    first = small_sum(net, s1_src, s1_slots, s1_out)
    step_of(first)

    slice_n = jnp.where(mask, dg(dg(hot, w_slice[...], 1, 0, EXACT), hot, 1, 1, EXACT), 0.0)
    n_hi, n_lo = split2(slice_n)
    bdd[:, 0:256] = n_hi
    bdd[:, 256:512] = n_hi
    bdd[:, 512:768] = n_lo
    wtc[...] = dg(hot, jnp.broadcast_to(w_temp[...], (128, 32)), 1, 1, EXACT)
    g2c[...] = jnp.broadcast_to(gain_two[...], (128, 256)).T
    hot4 = one_hot_rows(128)
    mask4 = same_block(128, 128)
    for i, w in enumerate((w_q, w_k, w_v)):
        bqkv[:, 128 * i : 128 * (i + 1)] = jnp.where(
            mask4, dg(dg(hot4, w[...], 1, 0, EXACT), hot4, 1, 1, EXACT), 0.0
        )
    for i in range(3, 7):
        loads[i].wait()
    wdT[...] = wd_v[...].T

    def hidden_gradient(i):
        s = pl.ds(pl.multiple_of(i * NB, NB), NB)
        cT[:, s] = cot_v[s, :].T
        dhT[:, s] = dg(wdT[...], cT[:, s], 1, 0)

    hidden_gradient(0)
    step_of(first)
    for i in range(1, chunks):
        hidden_gradient(i)
    woT[...] = wo_v[...].T
    wuT[...] = wu_v[...].T
    finish_of(first)

    total = s1_out[0:64, :]
    picked = []
    pick = (iota((32, 128), 1) % 32) == iota((32, 128), 0)
    for a in range(2):
        picked.append(jnp.where(pick, jnp.broadcast_to(s1_out[64 + a : 65 + a, :], (32, 128)), 0.0))
    ones4 = mask4.astype(F32)
    denb = dg(jnp.concatenate(picked, axis=0), ones4, 1, 0, EXACT) + EPS
    denb_s[...] = denb
    tok = total / denb
    tok_s[...] = tok
    qkv = dg(tok, bqkv[...], 1, 0, EXACT)
    qkv_s[...] = qkv
    scale = 32.0 ** (-0.5)
    mixT[...] = jnp.zeros_like(mixT)
    lhs_c[...] = jnp.zeros_like(lhs_c)
    for a in range(2):
        r = slice(32 * a, 32 * a + 32)
        q_a, k_a, v_a = qkv[r, 0:128], qkv[r, 128:256], qkv[r, 256:384]
        sc = dg(k_a, tile_diagonal(q_a), 1, 1, EXACT) * scale
        e = jnp.exp(sc - jnp.max(sc, axis=0, keepdims=True))
        pr = e / jnp.sum(e, axis=0, keepdims=True)
        prob_s[r, :] = pr
        m_t = jnp.where(mask4, dg(v_a, pr, 0, 0, EXACT), 0.0)
        block = slice(128 * a, 128 * a + 128)
        mixT[block, block] = m_t.astype(BF)
        lhs_c[block, block] = m_t.T.astype(BF)

    def rear(i, _):
        s = pl.ds(pl.multiple_of(i * NB, NB), NB)
        sp = dg(mixT[...], wb[:, s], 1, 0).astype(BF)
        sT[:, s] = sp
        res = (pT[:, s].astype(F32) + dg(woT[...], sp, 1, 0)).astype(BF).astype(F32)
        xc = res - jnp.sum(res, axis=0, keepdims=True) * (1.0 / C)
        var = jnp.sum(xc * xc, axis=0, keepdims=True) * (1.0 / C)
        rstd = lax.rsqrt(var + EPS)
        xhat = xc * rstd
        xh2[...] = xhat
        n2 = (xhat * lanes4(g2c[...])).astype(BF)
        n2T[:, s] = n2
        for f in range(FF // 256):
            fr = slice(256 * f, 256 * f + 256)
            pre = dg(wuT[fr, :], n2, 1, 0)
            x2 = pre * pre
            h = 0.5 + 0.5 * jnp.tanh(pre * (K0 + K1 * x2))
            hT[fr, s] = (pre * h).astype(BF)
            slope = h + (pre * (2.0 * K0 + (6.0 * K1) * x2)) * (h - h * h)
            dpT[fr, s] = (dhT[fr, s] * slope).astype(BF)
        dy = dg(wu_v[...], dpT[:, s], 1, 0)
        xhat = xh2[...]
        ga2[...] += fold_lanes(dy * xhat)
        dx = dy * lanes4(g2c[...])
        m1 = jnp.sum(dx, axis=0, keepdims=True) * (1.0 / C)
        m2 = jnp.sum(dx * xhat, axis=0, keepdims=True) * (1.0 / C)
        dr = cT[:, s].astype(F32) + rstd * (dx - m1 - xhat * m2)
        drT[:, s] = dr
        low = dr.astype(BF)
        drb[:, s] = low
        dsT[:, s] = dg(wo_v[...], low, 1, 0).astype(BF)
        return 0

    for i in range(chunks):
        rear(i, 0)
    s2_src[0:64, :] = fold_diagonal(dg(wb[...], dsT[...], 1, 1))
    s2_src[64:72, :] = jnp.zeros((8, 128), F32)
    second = small_sum(net, s2_src, s2_slots, s2_out)
    step_of(second)

    def put(left, right, at):
        v = dg(left, right, 1, 1)
        for j in range(v.shape[1] // 128):
            b_src[256 * (at + j) : 256 * (at + j + 1), :] = v[:, 128 * j : 128 * (j + 1)]

    bulk = bulk_sum(net, b_src, b_got0, b_sum0, b_got1, b_sum1, b_got2, b_slots, b_out)
    for f in range(4):
        fr = slice(256 * f, 256 * f + 256)
        put(n2T[...], dpT[fr, :], 2 * f)
        put(cT[...], hT[fr, :], 8 + 2 * f)
    put(sT[...], drb[...], 16)
    step_of(bulk)
    step_of(second)
    step_of(bulk)
    step_of(second)
    step_of(bulk)
    finish_of(second)

    dqs, dks, dvs = [], [], []
    for a in range(2):
        r = slice(32 * a, 32 * a + 32)
        q_a, k_a, v_a = qkv_s[r, 0:128], qkv_s[r, 128:256], qkv_s[r, 256:384]
        pr = prob_s[r, :]
        d_bd = tile_diagonal(s2_out[r, :])
        dvs.append(dg(pr, d_bd, 1, 0, EXACT))
        dp = dg(v_a, d_bd, 1, 1, EXACT)
        dsc = pr * (dp - jnp.sum(pr * dp, axis=0, keepdims=True)) * scale
        dq = jnp.where(mask4, dg(dsc, k_a, 0, 0, EXACT), 0.0)
        dqs.append(dq[0:32] + dq[32:64] + dq[64:96] + dq[96:128])
        dks.append(dg(dsc, tile_diagonal(q_a), 1, 0, EXACT))
    d_all = jnp.concatenate(
        [jnp.concatenate(v, axis=0) for v in (dqs, dks, dvs)], axis=1
    )
    d_tok = dg(d_all, bqkv[...], 1, 1, EXACT)
    tok = tok_s[...]
    d_num = d_tok / denb_s[...]
    d_den = -(d_num * tok)
    for a in range(2):
        r = slice(32 * a, 32 * a + 32)
        block = slice(128 * a, 128 * a + 128)
        bd = tile_diagonal(d_num[r])
        hi, lo = split2(bd)
        lhs_c[block, 256 + 128 * a : 384 + 128 * a] = hi
        lhs_c[block, 512 + 128 * a : 640 + 128 * a] = lo
        ddc[block, :] = jnp.broadcast_to(
            jnp.sum(tile_diagonal(d_den[r]), axis=1, keepdims=True), (128, 128)
        )
        hi_t, lo_t = split2(bd.T)
        dnT[block, :] = jnp.zeros((128, 512), BF)
        dnT[block, block] = hi_t
        dnT[block, 256 + 128 * a : 384 + 128 * a] = lo_t

    def finish(i):
        s = pl.ds(pl.multiple_of(i * NB, NB), NB)
        feats = mfT[256:512, s]
        dw = dg(lhs_c[...], jnp.concatenate([dsT[:, s], feats, feats], axis=0), 1, 0)
        sg, rt = sgs[:, s], rts[:, s]
        dts = []
        for h in range(HEADS):
            r = slice(32 * h, 32 * h + 32)
            w = ws[r, s]
            g = dw[r] + lanes4(ddc[r, :])
            d_l = w * (g - jnp.sum(w * g, axis=0, keepdims=True))
            inner = jnp.sum(d_l * ls[r, s], axis=0, keepdims=True)
            scale_h = rt[h : h + 1]
            dts.append(-(inner * scale_h) * sg[h : h + 1])
            hi, lo = split2(d_l * scale_h)
            dl_s[r, s] = hi
            dl_s[256 + 32 * h : 288 + 32 * h, s] = lo
        dt = jnp.concatenate(dts, axis=0)
        dt_hi = dt.astype(BF).astype(F32)
        dt_s[:, s] = jnp.concatenate([dt_hi, dt - dt_hi], axis=0).astype(BF)
        hi = dl_s[0:256, s]
        dm = dg(bdd[...], jnp.concatenate([hi, dl_s[256:512, s], hi], axis=0), 1, 0)
        for h in range(HEADS):
            r = slice(32 * h, 32 * h + 32)
            dmf_s[r, s] = (dm[r] + lanes4(wtc[r, :]) * dt[h : h + 1]).astype(BF)
        wbs = wb[:, s]
        dmf_s[256:512, s] = dg(dnT[...], jnp.concatenate([wbs, wbs], axis=0), 1, 0).astype(BF)

    def points_gradient(i):
        s = pl.ds(pl.multiple_of(i * NB, NB), NB)
        dy = dg(wmf[...], dmf_s[:, s], 1, 0)
        rstd = stat[1:2, s]
        xhat = (pT[:, s].astype(F32) - stat[0:1, s]) * rstd
        ga1[...] += fold_lanes(dy * xhat)
        dx = dy * lanes4(g1c[...])
        m1 = jnp.sum(dx, axis=0, keepdims=True) * (1.0 / C)
        m2 = jnp.sum(dx * xhat, axis=0, keepdims=True) * (1.0 / C)
        out = (drT[:, s] + rstd * (dx - m1 - xhat * m2)).astype(BF)
        gp_v[s, :] = out.T

    for i in range(chunks):
        finish(i)

    step_of(bulk)
    gmf = dg(nT[...], dmf_s[...], 1, 1)
    for j in range(4):
        t_src[256 * j : 256 * (j + 1), :] = gmf[:, 128 * j : 128 * (j + 1)]
    mids = mfT[0:256, :]
    gs = dg(mids, dl_s[0:256, :], 1, 1) + dg(mids, dl_s[256:512, :], 1, 1)
    gs64 = fold_diagonal(gs)
    t_src[1024:1056, :] = gs64[0:32] + gs64[32:64]
    gt = dg(mids, dt_s[...], 1, 1)
    gt = jnp.where(iota((256, 16), 1) % 8 == iota((256, 16), 0) // 32, gt, 0.0)
    gt = jnp.sum(gt, axis=1, keepdims=True)
    gt32 = gt[0:32]
    for h in range(1, HEADS):
        gt32 = gt32 + gt[32 * h : 32 * h + 32]
    t_src[1056:1088, :] = jnp.broadcast_to(gt32, (32, 128))
    tail = tail_sum(net, t_src, t_got, t_slots1, t_slots2, t_out)
    step_of(tail)
    for i in range(chunks):
        points_gradient(i)
    gain_rows = column_to_rows(jnp.sum(ga1[...], axis=1, keepdims=True)) + column_to_rows(
        jnp.sum(ga2[...], axis=1, keepdims=True)
    )
    s3_src[0:8, :] = jnp.concatenate(gain_rows + [jnp.zeros((4, 128), F32)], axis=0)
    s3_src[8:ROWS_S, :] = jnp.zeros((ROWS_S - 8, 128), F32)
    third = small_sum(net, s3_src, s3_slots, s3_out)
    step_of(third)
    step_of(bulk)
    step_of(tail)

    for i, d in enumerate((dqs, dks, dvs)):
        full = jnp.where(mask4, dg(tok, jnp.concatenate(d, axis=0), 0, 0, EXACT), 0.0)
        o_small[32 * i : 32 * (i + 1), :] = dg(hot4, full, 0, 0, EXACT)

    for _ in range(8):
        step_of(third)
        step_of(bulk)
        step_of(tail)
    o_small[96:104, :] = s3_out[0:8, :]
    o_small[104:168, :] = t_out[1024:1088, :]
    net.drain()


def unpack(
    gp, bulk, tail, small,
    o_points, o_mid, o_feat, o_out, o_up, o_down,
    o_one, o_two, o_slice, o_temp, o_q, o_k, o_v,
    sems,
):
    stores = [pltpu.make_async_copy(gp, o_points, sems.at[0])]
    stores[0].start()

    def store_columns(src, at, out, count, sem):
        for j in range(count):
            copy = pltpu.make_async_copy(
                src.at[pl.ds(256 * (at + j), 256), :],
                out.at[:, pl.ds(128 * j, 128)],
                sems.at[sem + j],
            )
            copy.start()
            stores.append(copy)

    store_columns(bulk, 0, o_up, 8, 1)
    store_columns(bulk, 8, o_down, 8, 9)
    store_columns(bulk, 16, o_out, 2, 17)
    store_columns(tail, 0, o_mid, 2, 19)
    store_columns(tail, 2, o_feat, 2, 21)
    hot4 = one_hot_rows(128)
    for i, o in enumerate((o_q, o_k, o_v)):
        o[...] = dg(small[32 * i : 32 * (i + 1), :], hot4, 1, 0, EXACT)
    o_slice[...] = dg(small[104:136, :], hot4, 1, 0, EXACT)
    diag = iota((32, 128), 0) == iota((32, 128), 1)
    o_temp[...] = jnp.sum(jnp.where(diag, small[136:168, :], 0.0), axis=0, keepdims=True)[:, 0:32]
    o_one[:, 0:128] = small[96:97, :]
    o_one[:, 128:256] = small[97:98, :]
    o_two[:, 0:128] = small[98:99, :]
    o_two[:, 128:256] = small[99:100, :]
    for store in stores:
        store.wait()


def call(active, n, args):
    (points, cotangent, gain_one, gain_two, w_mid, w_feat, w_out, w_up, w_down,
     w_slice, w_temp, w_q, w_k, w_v) = args
    vm = lambda *shape: pltpu.VMEM(shape, F32)
    vb = lambda *shape: pltpu.VMEM(shape, BF)
    any_spec = pl.BlockSpec(memory_space=pl.ANY)
    vmem_spec = pl.BlockSpec(memory_space=pltpu.VMEM)
    out_shape = (
        [jax.ShapeDtypeStruct((n, C), BF)]
        + [jax.ShapeDtypeStruct((C, C), F32)] * 3
        + [jax.ShapeDtypeStruct((C, FF), F32)] * 2
        + [jax.ShapeDtypeStruct((1, C), F32)] * 2
        + [jax.ShapeDtypeStruct((32, 32), F32), jax.ShapeDtypeStruct((1, 32), F32)]
        + [jax.ShapeDtypeStruct((32, 32), F32)] * 3
    )
    small = [vm(ROWS_S, 128), vm(48 * PART_S, 128), vm(ROWS_S, 128)]
    scratch = (
        [vb(n, C), vb(n, C), vb(C, C), vb(C, C), vb(C, C), vb(C, FF), vb(C, FF)]
        + [vb(C, n), vb(C, n), vb(512, C), vb(C, 512), vb(C, C), vb(FF, C), vb(FF, C)]
        + [vm(C, 128), vm(C, 128), vm(C, 128), vb(800, C), vb(C, 768), vm(128, 384)]
        + [vm(8, n), vb(C, n), vb(512, n), vm(8, n), vm(8, n), vm(C, n), vm(C, n), vb(C, n), vm(C, 128)]
        + [vm(64, 128), vm(64, 384), vm(64, 128), vm(64, 128), vb(C, C), vb(C, 768), vb(C, 512), vm(C, 128)]
        + [vm(FF, n), vb(C, n), vb(C, n), vm(C, NB), vb(FF, n), vb(FF, n), vm(C, n), vb(C, n), vb(C, n),
           vm(C, 128), vm(C, 128)]
        + [vb(512, n), vb(16, n), vb(512, n)]
        + small
        + small
        + small
        + [vm(ROWS_G, 128), vm(2304, 128), vm(2304, 128), vm(9 * 192, 128), vm(576, 128), vm(9 * 48, 128),
           vm(12 * 48, 128)]
        + [vm(ROWS_T, 128), vm(24 * 48, 128), vm(12 * 48, 128), vm(12 * 48, 128)]
        + [pltpu.SemaphoreType.DMA((7,)),
           pltpu.SemaphoreType.DMA((256,)), pltpu.SemaphoreType.DMA((256,))]
    )

    def body(*refs):
        kernel(active, *refs)

    mid_shape = [pltpu.VMEM((n, C), BF), pltpu.VMEM((ROWS_G, 128), F32), pltpu.VMEM((ROWS_T, 128), F32),
                 pltpu.VMEM((168, 128), F32)]
    packed = pl.pallas_call(
        body,
        name="block_backward",
        out_shape=mid_shape,
        in_specs=[any_spec] * 7 + [vmem_spec] * 7,
        out_specs=[vmem_spec] * 4,
        scratch_shapes=scratch,
        compiler_params=pltpu.CompilerParams(
            vmem_limit_bytes=56 * 2**20,
            has_side_effects=True,
            **({"collective_id": 0} if active else {}),
        ),
    )(
        points, cotangent, w_mid, w_feat, w_out, w_up, w_down,
        gain_one.reshape(1, C), gain_two.reshape(1, C), w_slice, w_temp.reshape(1, 32), w_q, w_k, w_v,
    )
    outs = pl.pallas_call(
        unpack,
        name="unpack",
        out_shape=out_shape,
        in_specs=[vmem_spec] * 4,
        out_specs=[any_spec] * 6 + [vmem_spec] * 7,
        scratch_shapes=[pltpu.SemaphoreType.DMA((23,))],
        compiler_params=pltpu.CompilerParams(vmem_limit_bytes=4 * 2**20),
    )(*packed)
    outs = list(outs)
    outs[6], outs[7], outs[9] = outs[6].reshape(C), outs[7].reshape(C), outs[9].reshape(32)
    return tuple(outs)


def solution(mesh):
    rows_spec = P(("pts", "grp"), None)

    def local(*args):
        return call(True, args[0].shape[0], args)

    return jax.shard_map(
        local,
        mesh=mesh,
        in_specs=(rows_spec, rows_spec) + (P(),) * 12,
        out_specs=(rows_spec,) + (P(),) * 12,
        check_vma=False,
    )
```
